512 devices in a mesh: dp: 2 (over x_lo), seq: 32 (over z, core), tensor: 8 (over y, x_hi).
Axes of the slice: x: 4 (x_hi: 2, x_lo: 2; x = x_hi * 2 + x_lo), y: 4, z: 16, core: 2. Of those that a mesh axis runs over, the one named last changes fastest.
Arguments:
- queries: bfloat16 [2, 4096, 3072], P('dp', 'seq', 'tensor'), may hold values from -24 to 24
- keys: bfloat16 [2, 8192, 3072], P('dp', 'seq', 'tensor'), may hold values from -8 to 8
- values: bfloat16 [2, 8192, 3072], P('dp', 'seq', 'tensor'), may hold values from -160 to 160
- grad_out: bfloat16 [2, 4096, 3072], P('dp', 'seq', 'tensor'), may hold values from -60 to 60
- gain: float32 [3072], P('tensor'), may hold values from 0.1 to 1.9
- band_start: int32 [2, 32], P('dp', 'seq'), may hold values from 0 to 62, as said below
- band_end: int32 [2, 32], P('dp', 'seq'), may hold values from 6 to 64
Outputs:
- attended: bfloat16 [2, 4096, 3072], P('dp', 'seq', 'tensor')
- grad_queries: bfloat16 [2, 4096, 3072], P('dp', 'seq', 'tensor')
- grad_keys: bfloat16 [2, 8192, 3072], P('dp', 'seq', 'tensor')
- grad_values: bfloat16 [2, 8192, 3072], P('dp', 'seq', 'tensor')
- grad_gain: float32 [3072], P('tensor')
The draws below stay inside these ranges and needn't reach their ends.
Inputs may be any that keep to these rules, and one draw needn't show every extreme that they name: Along the token blocks of a recording band_start and band_end never fall and band_start < band_end; the band of a token block held by seq index j lies within encoder blocks (j - 2) * (2) to (j + 3) * 2 - 1, and in every draw some bands reach both of these limits.
All inputs are finite; a program needn't handle non-finite values.
Results may differ from the reference program's by a relative error of at most 0.008.
Values may be sent and summed in bfloat16 or wider, within the bound.
No kernel may reach another device: no remote copies, remote signals or barrier semaphores. Data moves between devices by JAX's collectives and lax.ppermute only.
A program may use at most 64 MiB of HBM per device.

```python
import math
import jax
import jax.numpy as jnp
from jax import lax

D = 3072
HD = 96
TOK_DEV = 128
F_DEV = 256
TB = 128
EB = 128
REACH = 2
REC = 2
TOKENS = 4096
FRAMES = 8192
NTB = 32
NEB = 64


def draw_queries(key, part):
    key = jax.random.fold_in(key, 101)
    shape = (REC, TOKENS, D)
    base = jax.random.truncated_normal(key, -6.0, 6.0, shape, jnp.float32)
    return base.astype(jnp.bfloat16)


def draw_keys(key, part):
    key = jax.random.fold_in(key, 202)
    shape = (REC, FRAMES, D)
    base = jax.random.truncated_normal(key, -6.0, 6.0, shape, jnp.float32)
    return base.astype(jnp.bfloat16)


def draw_values(key, part):
    key = jax.random.fold_in(key, 303)
    shape = (REC, FRAMES, D)
    key_col = jax.random.fold_in(key, 0)
    key_base = jax.random.fold_in(key, 2)
    column_scale = jnp.exp(jax.random.uniform(key_col, (D,), jnp.float32, 0.0, math.log(10.0)))
    base = jax.random.truncated_normal(key_base, -6.0, 6.0, shape, jnp.float32)
    return (base * column_scale[None, None, :]).astype(jnp.bfloat16)


def draw_grad_out(key, part):
    key = jax.random.fold_in(key, 404)
    shape = (REC, TOKENS, D)
    key_row, key_base = jax.random.split(key, 2)
    row_scale = jnp.exp(jax.random.uniform(key_row, (REC, TOKENS, 1), jnp.float32, 0.0, math.log(10.0)))
    position = jnp.arange(TOKENS, dtype=jnp.float32)[None, :, None] / TOKENS
    base = jax.random.truncated_normal(key_base, -6.0, 6.0, shape, jnp.float32)
    ramp = jnp.exp(position * math.log(3.0))
    return (0.3 * base * row_scale * ramp).astype(jnp.bfloat16)


def band_pair(key):
    shared = jax.random.fold_in(key, 11)
    key_limit, key_low, key_high = jax.random.split(shared, 3)
    per_device = TOK_DEV // TB
    per_encoder = F_DEV // EB
    devices = NTB // per_device
    block = jnp.arange(NTB, dtype=jnp.int32)
    center = block * NEB // NTB
    device = block // per_device
    lowest = jnp.maximum((device - REACH) * per_encoder, 0)
    highest = jnp.minimum((device + REACH + 1) * per_encoder, NEB)
    full = (REACH + 1) * per_encoder
    limit = jax.random.randint(key_limit, (REC, devices), 1, full + 1, jnp.int32)
    limit = jnp.repeat(limit, per_device, axis=1)
    below = jax.random.randint(key_low, (REC, NTB), 0, 1 << 20, jnp.int32) % (limit + 1)
    above = jax.random.randint(key_high, (REC, NTB), 0, 1 << 20, jnp.int32) % (limit + 1)
    forced = block % 7 == 0
    last = block == NTB - 1
    below = jnp.where(forced[None, :], full, below)
    above = jnp.where(forced[None, :] | last[None, :], full, above)
    below = jnp.where(last[None, :], 0, below)
    start = jnp.maximum(lax.cummax(center[None, :] - below, axis=1), lowest[None, :])
    finish = jnp.minimum(lax.cummax(center[None, :] + 1 + above, axis=1), highest[None, :])
    return (start.astype(jnp.int32), finish.astype(jnp.int32))


def draw_band_start(key, part):
    return band_pair(key)[0]


def draw_band_end(key, part):
    return band_pair(key)[1]


def setup_inputs(seed: int = 0) -> dict:
    streams_of = jax.random.split(jax.random.key(seed), 8)
    return {
        "queries": draw_queries(jax.random.fold_in(streams_of[7], 71), 0),
        "keys": draw_keys(jax.random.fold_in(streams_of[7], 71), 0),
        "values": draw_values(jax.random.fold_in(streams_of[7], 71), 0),
        "grad_out": draw_grad_out(jax.random.fold_in(streams_of[7], 71), 0),
        "gain": jnp.clip(1.0 + 0.18 * jax.random.normal(streams_of[4], (D,), jnp.float32), 0.1, 1.9),
        "band_start": draw_band_start(jax.random.fold_in(streams_of[7], 71), 0),
        "band_end": draw_band_end(jax.random.fold_in(streams_of[7], 71), 0),
    }


epsilon = 1e-06

def reference(queries, keys, values, grad_out, gain, band_start, band_end):
    heads = D // HD
    scale = HD ** (-0.5)
    span = (2 * REACH + 1) * F_DEV
    per_device = TOK_DEV // TB
    margin = REACH * F_DEV
    attended_all = []
    grad_query_all = []
    grad_key_all = []
    grad_value_all = []
    gain_total = jnp.zeros((D,), jnp.float32)
    for record in range(REC):
        query_rec = queries[record]
        key_pad = jnp.pad(keys[record], ((margin, margin), (0, 0)))
        value_pad = jnp.pad(values[record], ((margin, margin), (0, 0)))
        grad_rec = grad_out[record]
        starts = band_start[record]
        ends = band_end[record]

        def block_step(carry, block):
            key_acc, value_acc, gain_acc = carry
            device = block // per_device
            first = (device * F_DEV).astype(jnp.int32)
            row_first = (block * TB).astype(jnp.int32)
            query_block = lax.dynamic_slice_in_dim(query_rec, row_first, TB, 0)
            grad_block = lax.dynamic_slice_in_dim(grad_rec, row_first, TB, 0).astype(jnp.float32)
            key_block = lax.dynamic_slice_in_dim(key_pad, first, span, 0)
            value_block = lax.dynamic_slice_in_dim(value_pad, first, span, 0)
            frame_block = ((device - REACH) * F_DEV + jnp.arange(span, dtype=jnp.int32)) // EB
            allowed = (frame_block >= starts[block]) & (frame_block < ends[block])
            query_heads = query_block.astype(jnp.float32).reshape(TB, heads, HD)
            key_heads = key_block.astype(jnp.float32).reshape(span, heads, HD)
            value_heads = value_block.astype(jnp.float32).reshape(span, heads, HD)
            scores = jnp.einsum('qhd,khd->hqk', query_heads, key_heads) * scale
            scores = jnp.where(allowed[None, None, :], scores, -jnp.inf)
            top = lax.optimization_barrier(jnp.max(scores, axis=-1, keepdims=True))
            weights = jnp.exp(scores - top)
            probs = weights / lax.optimization_barrier(jnp.sum(weights, axis=-1, keepdims=True))
            probs_b = lax.optimization_barrier(probs.astype(jnp.bfloat16)).astype(jnp.float32)
            attn = jnp.einsum('hqk,khd->qhd', probs_b, value_heads).reshape(TB, D)
            inv_rms = lax.rsqrt(lax.optimization_barrier(jnp.mean(attn * attn, axis=1)) + epsilon)
            normed = attn * inv_rms[:, None]
            attended = (normed * gain[None, :]).astype(jnp.bfloat16)
            gain_acc = gain_acc + lax.optimization_barrier(jnp.sum(grad_block * normed, axis=0))
            scaled_grad = grad_block * gain[None, :]
            mean_cross = lax.optimization_barrier(jnp.mean(scaled_grad * normed, axis=1))
            grad_attn = (inv_rms[:, None] * (scaled_grad - normed * mean_cross[:, None])).astype(jnp.bfloat16)
            grad_attn_heads = lax.optimization_barrier(grad_attn).astype(jnp.float32).reshape(TB, heads, HD)
            grad_probs = jnp.einsum('qhd,khd->hqk', grad_attn_heads, value_heads)
            inner = lax.optimization_barrier(jnp.sum(probs * grad_probs, axis=-1, keepdims=True))
            grad_scores = lax.optimization_barrier((probs * (grad_probs - inner)).astype(jnp.bfloat16)).astype(jnp.float32)
            grad_query = (scale * jnp.einsum('hqk,khd->qhd', grad_scores, key_heads)).reshape(TB, D).astype(jnp.bfloat16)
            grad_key = (scale * jnp.einsum('hqk,qhd->khd', grad_scores, query_heads)).reshape(span, D)
            grad_value = jnp.einsum('hqk,qhd->khd', probs_b, grad_attn_heads).reshape(span, D)
            key_acc = lax.dynamic_update_slice_in_dim(key_acc, lax.dynamic_slice_in_dim(key_acc, first, span, 0) + grad_key, first, 0)
            value_acc = lax.dynamic_update_slice_in_dim(value_acc, lax.dynamic_slice_in_dim(value_acc, first, span, 0) + grad_value, first, 0)
            return ((key_acc, value_acc, gain_acc), (attended, grad_query))
        start_carry = (jnp.zeros((FRAMES + 2 * margin, D), jnp.float32), jnp.zeros((FRAMES + 2 * margin, D), jnp.float32), jnp.zeros((D,), jnp.float32))
        final, stacked = lax.scan(block_step, start_carry, jnp.arange(NTB, dtype=jnp.int32))
        key_acc, value_acc, gain_acc = final
        gain_total = gain_total + gain_acc
        attended_all.append(stacked[0].reshape(TOKENS, D))
        grad_query_all.append(stacked[1].reshape(TOKENS, D))
        grad_key_all.append(key_acc[margin:margin + FRAMES].astype(jnp.bfloat16))
        grad_value_all.append(value_acc[margin:margin + FRAMES].astype(jnp.bfloat16))
    return (jnp.stack(attended_all), jnp.stack(grad_query_all), jnp.stack(grad_key_all), jnp.stack(grad_value_all), gain_total)
```

```python
import jax
import jax.numpy as jnp
from jax import lax
from jax.experimental import pallas as pl
from jax.experimental.pallas import tpu as pltpu
from jax.sharding import PartitionSpec as P

D = 3072
HD = 96
TB = 128
EB = 128
FR = 256
W = 384
TENSOR = 8
SEQ = 32
SCALE = HD ** (-0.5)
epsilon = 1e-06

PIECES = 5
NT = (((1,), (1,)), ((), ()))
TN = (((0,), (0,)), ((), ()))
PAIRS = ((0, (0, 96)), (128, (64, 160)))


def permute(array, axis, target):
    size = lax.axis_size(axis)
    pairs = [(i, target(i)) for i in range(size) if 0 <= target(i) < size]
    return lax.ppermute(array, axis, pairs)


def offsets(here):
    core = lax.rem(here, 2)
    toward = 1 - 2 * core
    return (0, toward, -2, 2, -toward)


def blocked(rows, pair):
    first, starts = PAIRS[pair]
    part = rows[:, first : first + 256]
    lane = lax.broadcasted_iota(jnp.int32, part.shape, 1)
    zero = jnp.zeros_like(part)
    return jnp.concatenate(
        [jnp.where((lane >= at) & (lane < at + HD), part, zero) for at in starts], axis=0
    )


def side_by_side(pairs):
    lane = lax.broadcasted_iota(jnp.int32, (TB, 256), 1)
    low = jnp.where(lane < HD, pairs[0][:TB], pairs[0][TB:])
    high = jnp.where(lane < 160, pairs[1][:TB], pairs[1][TB:])
    middle = jnp.where(lane[:, :128] < 64, low[:, 128:], high[:, :128])
    return jnp.concatenate([low[:, :128], middle, high[:, 128:]], axis=1)


def to_rows(columns):
    lane = lax.broadcasted_iota(jnp.int32, (TB, TB), 1)
    tile = jnp.zeros((TB, TB), jnp.float32)
    for index, column in enumerate(columns):
        tile = jnp.where(lane == index, column, tile)
    return tile.T


def forward_kernel(
    start_ref, end_ref, q_ref, go_ref, gain_ref, *rest
):
    pieces = rest[:PIECES]
    attn_ref, probs_ref, stats_ref, scores = rest[PIECES:]
    here = lax.axis_index("seq")
    first = start_ref[0, 0]
    last = end_ref[0, 0]
    rows = q_ref[...]
    results = []
    for pair in range(2):
        at = PAIRS[pair][0]
        block = blocked(rows, pair)
        top = None
        for index, offset in enumerate(offsets(here)):
            frames = 2 * (here + offset)
            product = (
                lax.dot_general(
                    block,
                    pieces[index][0:FR, at : at + 256],
                    NT,
                    preferred_element_type=jnp.float32,
                )
                * SCALE
            )
            for half in range(2):
                allowed = (frames + half >= first) & (frames + half < last)
                bias = jnp.where(allowed, 0.0, -jnp.inf)
                part = product[:, half * EB : (half + 1) * EB] + bias
                scores[pair, :, index * FR + half * EB : index * FR + (half + 1) * EB] = part
                top = part if top is None else jnp.maximum(top, part)
        top = jnp.max(top, axis=1, keepdims=True)
        weights = jnp.exp(scores[pair] - top)
        total = jnp.sum(weights, axis=1, keepdims=True)
        probs = weights * (1.0 / total)
        probs_ref[pair] = probs
        probs = probs.astype(jnp.bfloat16)
        acc = None
        for index in range(PIECES):
            part = jnp.dot(
                probs[:, index * FR : (index + 1) * FR],
                pieces[index][FR : 2 * FR, at : at + 256],
                preferred_element_type=jnp.float32,
            )
            acc = part if acc is None else acc + part
        results.append(acc)
    attn = side_by_side(results)
    attn_ref[...] = attn
    scaled = go_ref[...].astype(jnp.float32) * gain_ref[...]
    square = jnp.sum(attn * attn, axis=1, keepdims=True)
    cross = jnp.sum(scaled * attn, axis=1, keepdims=True)
    stats = to_rows([square, cross])[0:2]
    for index in range(TENSOR):
        stats_ref[index] = stats


def backward_kernel(q_ref, go_ref, gain_ref, attn_ref, probs_ref, stats_ref, *rest):
    pieces = rest[:PIECES]
    attended_ref, gain_part_ref, gq_ref, own_ref = rest[PIECES : PIECES + 4]
    outs = rest[PIECES + 4 : PIECES + 8]
    grads = rest[PIECES + 8]
    stats = stats_ref[0]
    for index in range(1, TENSOR):
        stats = stats + stats_ref[index]
    row = lax.broadcasted_iota(jnp.int32, (TB, TB), 0)
    tile = jnp.where(row == 0, stats[0:1], jnp.where(row == 1, stats[1:2], 0.0)).T
    inv = lax.rsqrt(tile[:, 0:1] / D + epsilon)
    mean_cross = inv * tile[:, 1:2] / D
    grad = go_ref[...].astype(jnp.float32)
    gain = gain_ref[...]
    normed = attn_ref[...] * inv
    attended_ref[...] = (normed * gain).astype(jnp.bfloat16)
    gain_part_ref[...] = jnp.sum(grad * normed, axis=0, keepdims=True)
    grad_attn = (inv * (grad * gain - normed * mean_cross)).astype(jnp.bfloat16)
    rows = q_ref[...]
    grad_q = []
    grad_kv = [[None, None] for _ in range(PIECES)]
    for pair in range(2):
        at = PAIRS[pair][0]
        block = blocked(rows, pair)
        cot = blocked(grad_attn, pair)
        inner = None
        for index in range(PIECES):
            part = lax.dot_general(
                cot,
                pieces[index][FR : 2 * FR, at : at + 256],
                NT,
                preferred_element_type=jnp.float32,
            )
            grads[:, index * FR : (index + 1) * FR] = part
            part = probs_ref[pair, :, index * FR : (index + 1) * FR] * part
            inner = part if inner is None else inner + part
        inner = jnp.sum(inner, axis=1, keepdims=True)
        acc = None
        for index in range(PIECES):
            span = slice(index * FR, (index + 1) * FR)
            probs = probs_ref[pair, :, span]
            ds = (probs * (grads[:, span] - inner)).astype(jnp.bfloat16)
            part = jnp.dot(
                ds, pieces[index][0:FR, at : at + 256], preferred_element_type=jnp.float32
            )
            acc = part if acc is None else acc + part
            gk = lax.dot_general(ds, block, TN, preferred_element_type=jnp.float32) * SCALE
            gv = lax.dot_general(
                probs.astype(jnp.bfloat16), cot, TN, preferred_element_type=jnp.float32
            )
            out = own_ref if index == 0 else outs[index - 1]
            for base, value in ((0, gk), (FR, gv)):
                span_rows = slice(base, base + FR)
                if pair == 0:
                    out[span_rows, 0:128] = value[:, 0:128].astype(out.dtype)
                    grad_kv[index][base // FR] = value[:, 128:256]
                else:
                    middle = grad_kv[index][base // FR] + value[:, 0:128]
                    out[span_rows, 128:256] = middle.astype(out.dtype)
                    out[span_rows, 256:384] = value[:, 128:256].astype(out.dtype)
        grad_q.append(acc)
    gq_ref[...] = (side_by_side(grad_q) * SCALE).astype(jnp.bfloat16)


VMEM = pl.BlockSpec(memory_space=pltpu.VMEM)
SMEM = pl.BlockSpec(memory_space=pltpu.SMEM)


def per_device(queries, keys, values, grad_out, gain, band_start, band_end):
    f32, bf16 = jnp.float32, jnp.bfloat16
    here = lax.axis_index("seq")
    core = lax.rem(here, 2)
    own = jnp.concatenate([keys[0], values[0]], axis=0)
    below = permute(own, "seq", lambda i: i + 2)
    above = permute(own, "seq", lambda i: i - 2)
    partner = permute(own, "seq", lambda i: i ^ 1)
    beyond = permute(jnp.where(core == 0, above, below), "seq", lambda i: i ^ 1)
    pieces = (own, partner, below, above, beyond)
    query = queries[0]
    grad = grad_out[0]
    gain_row = gain[None]
    attn, probs, stats = pl.pallas_call(
        forward_kernel,
        out_shape=(
            jax.ShapeDtypeStruct((TB, W), f32),
            jax.ShapeDtypeStruct((2, 2 * TB, PIECES * FR), f32),
            jax.ShapeDtypeStruct((TENSOR, 2, TB), f32),
        ),
        in_specs=[SMEM, SMEM] + [VMEM] * (3 + PIECES),
        out_specs=(VMEM, VMEM, VMEM),
        scratch_shapes=[pltpu.VMEM((2, 2 * TB, PIECES * FR), f32)],
        name="attention_forward",
    )(band_start, band_end, query, grad, gain_row, *pieces)
    stats = lax.all_to_all(stats, "tensor", 0, 0, tiled=False)
    back = pl.pallas_call(
        backward_kernel,
        out_shape=(
            jax.ShapeDtypeStruct((TB, W), bf16),
            jax.ShapeDtypeStruct((1, W), f32),
            jax.ShapeDtypeStruct((TB, W), bf16),
            jax.ShapeDtypeStruct((2 * FR, W), f32),
        )
        + (jax.ShapeDtypeStruct((2 * FR, W), bf16),) * 4,
        in_specs=[VMEM] * (6 + PIECES),
        out_specs=(VMEM,) * 8,
        scratch_shapes=[pltpu.VMEM((2 * TB, PIECES * FR), f32)],
        name="attention_backward",
    )(query, grad, gain_row, attn, probs, stats, *pieces)
    attended, gain_part, grad_queries, total, to_partner, to_below, to_above, to_beyond = back
    got = [
        permute(to_below, "seq", lambda i: i - 2),
        permute(to_above, "seq", lambda i: i + 2),
        permute(to_beyond, "seq", lambda i: i - 1 if i % 2 == 0 else i + 1),
        permute(to_partner, "seq", lambda i: i ^ 1),
    ]
    gain_pair = gain_part + lax.ppermute(gain_part, "dp", [(0, 1), (1, 0)])
    spread = lax.all_to_all(
        jnp.broadcast_to(gain_pair, (SEQ, W)), "seq", 0, 0, tiled=True
    )
    grad_gain = jnp.sum(spread, axis=0)
    for part in got:
        total = total + part.astype(f32)
    total = total.astype(bf16)
    return (
        attended[None],
        grad_queries[None],
        total[None, :FR],
        total[None, FR:],
        grad_gain,
    )


def solution(mesh):
    return jax.shard_map(
        per_device,
        mesh=mesh,
        in_specs=(
            P("dp", "seq", "tensor"),
            P("dp", "seq", "tensor"),
            P("dp", "seq", "tensor"),
            P("dp", "seq", "tensor"),
            P("tensor"),
            P("dp", "seq"),
            P("dp", "seq"),
        ),
        out_specs=(
            P("dp", "seq", "tensor"),
            P("dp", "seq", "tensor"),
            P("dp", "seq", "tensor"),
            P("dp", "seq", "tensor"),
            P("tensor"),
        ),
        check_vma=False,
    )
```

```python
import jax
import jax.numpy as jnp
from jax import lax
from jax.experimental import pallas as pl
from jax.experimental.pallas import tpu as pltpu
from jax.sharding import PartitionSpec as P


D = 3072
HD = 96
TB = 128
EB = 128
FR = 256
W = 384
TENSOR = 8
SEQ = 32
SCALE = HD ** (-0.5)
epsilon = 1e-06

PIECES = 5
NT = (((1,), (1,)), ((), ()))
PAIRS = ((0, (0, 96)), (128, (64, 160)))


def permute(array, axis, target):
    size = lax.axis_size(axis)
    pairs = [(i, target(i)) for i in range(size) if 0 <= target(i) < size]
    return lax.ppermute(array, axis, pairs)


def offsets(here):
    core = lax.rem(here, 2)
    toward = 1 - 2 * core
    return (0, toward, -2, 2, -toward)


def blocked(rows, pair):
    first, starts = PAIRS[pair]
    part = rows[:, first : first + 256]
    lane = lax.broadcasted_iota(jnp.int32, part.shape, 1)
    zero = jnp.zeros_like(part)
    return jnp.concatenate(
        [jnp.where((lane >= at) & (lane < at + HD), part, zero) for at in starts], axis=0
    )


def side_by_side(pairs):
    lane = lax.broadcasted_iota(jnp.int32, (TB, 256), 1)
    low = jnp.where(lane < HD, pairs[0][:TB], pairs[0][TB:])
    high = jnp.where(lane < 160, pairs[1][:TB], pairs[1][TB:])
    middle = jnp.where(lane[:, :128] < 64, low[:, 128:], high[:, :128])
    return jnp.concatenate([low[:, :128], middle, high[:, 128:]], axis=1)


def to_rows(columns):
    lane = lax.broadcasted_iota(jnp.int32, (TB, TB), 1)
    tile = jnp.zeros((TB, TB), jnp.float32)
    for index, column in enumerate(columns):
        tile = jnp.where(lane == index, column, tile)
    return tile.T


def split(rows):
    terms = []
    for _ in range(3):
        term = rows.astype(jnp.bfloat16)
        rows = rows - term.astype(jnp.float32)
        terms.append(term)
    return jnp.concatenate(terms, axis=1)


def merge(terms):
    terms = terms.astype(jnp.float32)
    return (terms[:, 0:TB] + terms[:, TB : 2 * TB]) + terms[:, 2 * TB : W]


def pack_kernel(
    k_ref, v_ref, q_ref, go_ref, gain_ref, own_ref, query_ref, grad_ref, row_ref, line, sems
):
    moves = (
        (k_ref, own_ref.at[0:FR]),
        (v_ref, own_ref.at[FR : 2 * FR]),
        (q_ref, query_ref),
        (go_ref, grad_ref),
        (gain_ref, line),
    )
    copies = [
        pltpu.make_async_copy(source, target, sems.at[index])
        for index, (source, target) in enumerate(moves)
    ]
    for copy in copies:
        copy.start()
    for copy in copies:
        copy.wait()
    row_ref[...] = line[...].reshape(1, W)


def forward_kernel(
    start_ref, end_ref, q_ref, go_ref, gain_ref, *rest
):
    pieces = rest[:PIECES]
    attn_ref, probs_ref, stats_ref, norms_ref, scores = rest[PIECES:]
    here = lax.axis_index("seq")
    first = start_ref[0, 0]
    last = end_ref[0, 0]
    rows = q_ref[...]
    results = []
    tops = []
    scales = []
    for pair in range(2):
        at = PAIRS[pair][0]
        block = blocked(rows, pair)
        top = None
        for index, offset in enumerate(offsets(here)):
            frames = 2 * (here + offset)
            product = (
                lax.dot_general(
                    block,
                    pieces[index][0:FR, at : at + 256],
                    NT,
                    preferred_element_type=jnp.float32,
                )
                * SCALE
            )
            for half in range(2):
                allowed = (frames + half >= first) & (frames + half < last)
                bias = jnp.where(allowed, 0.0, -jnp.inf)
                part = product[:, half * EB : (half + 1) * EB] + bias
                scores[pair, :, index * FR + half * EB : index * FR + (half + 1) * EB] = part
                top = part if top is None else jnp.maximum(top, part)
        top = jnp.max(top, axis=1, keepdims=True)
        weights = jnp.exp(scores[pair] - top)
        total = jnp.sum(weights, axis=1, keepdims=True)
        inverse = 1.0 / total
        tops += [top[:TB], top[TB:]]
        scales += [inverse[:TB], inverse[TB:]]
        probs = weights * inverse
        probs_ref[pair] = probs
        probs = probs.astype(jnp.bfloat16)
        acc = None
        for index in range(PIECES):
            part = jnp.dot(
                probs[:, index * FR : (index + 1) * FR],
                pieces[index][FR : 2 * FR, at : at + 256],
                preferred_element_type=jnp.float32,
            )
            acc = part if acc is None else acc + part
        results.append(acc)
    attn = side_by_side(results)
    attn_ref[...] = attn
    scaled = go_ref[...].astype(jnp.float32) * gain_ref[...]
    square = jnp.sum(attn * attn, axis=1, keepdims=True)
    cross = jnp.sum(scaled * attn, axis=1, keepdims=True)
    stats = to_rows([*tops, *scales, square, cross])
    norms_ref[...] = stats[0:8]
    for index in range(TENSOR):
        stats_ref[index] = stats[8:10]


def token_kernel(
    start_ref, end_ref, q_ref, go_ref, gain_ref, attn_ref, probs_ref, norms_ref, stats_ref, *rest
):
    pieces = rest[:PIECES]
    attended_ref, gain_part_ref, gq_ref, sent_ref, grads = rest[PIECES:]
    stats = stats_ref[0]
    for index in range(1, TENSOR):
        stats = stats + stats_ref[index]
    row = lax.broadcasted_iota(jnp.int32, (TB, TB), 0)
    tile = jnp.where(row == 0, stats[0:1], jnp.where(row == 1, stats[1:2], 0.0)).T
    inv = lax.rsqrt(tile[:, 0:1] / D + epsilon)
    mean_cross = inv * tile[:, 1:2] / D
    grad = go_ref[...].astype(jnp.float32)
    gain = gain_ref[...]
    normed = attn_ref[...] * inv
    attended_ref[...] = (normed * gain).astype(jnp.bfloat16)
    gain_part_ref[...] = jnp.broadcast_to(
        jnp.sum(grad * normed, axis=0, keepdims=True)[None], (SEQ, 1, W)
    )
    grad_attn = (inv * (grad * gain - normed * mean_cross)).astype(jnp.bfloat16)
    rows = q_ref[...]
    sent_ref[0:TB] = grad_attn
    sent_ref[TB : 2 * TB] = rows
    grad_q = []
    inners = []
    for pair in range(2):
        at = PAIRS[pair][0]
        cot = blocked(grad_attn, pair)
        inner = None
        for index in range(PIECES):
            span = slice(index * FR, (index + 1) * FR)
            part = lax.dot_general(
                cot,
                pieces[index][FR : 2 * FR, at : at + 256],
                NT,
                preferred_element_type=jnp.float32,
            )
            grads[:, span] = part
            part = probs_ref[pair, :, span] * part
            inner = part if inner is None else inner + part
        inner = jnp.sum(inner, axis=1, keepdims=True)
        inners += [inner[:TB], inner[TB:]]
        acc = None
        for index in range(PIECES):
            span = slice(index * FR, (index + 1) * FR)
            ds = (probs_ref[pair, :, span] * (grads[:, span] - inner)).astype(jnp.bfloat16)
            part = jnp.dot(
                ds, pieces[index][0:FR, at : at + 256], preferred_element_type=jnp.float32
            )
            acc = part if acc is None else acc + part
        grad_q.append(acc)
    gq_ref[...] = (side_by_side(grad_q) * SCALE).astype(jnp.bfloat16)
    band = lax.broadcasted_iota(jnp.int32, (4, TB), 0)
    band = jnp.where(band == 0, start_ref[0, 0], end_ref[0, 0]).astype(jnp.float32)
    sent_ref[2 * TB : 2 * TB + 16] = split(
        jnp.concatenate([norms_ref[...], to_rows(inners)[0:4], band], axis=0)
    )


def frame_kernel(own_ref, *rest):
    tokens = rest[:PIECES]
    gk_ref, gv_ref = rest[PIECES:]
    here = lax.axis_index("seq")
    totals = []
    extras = [merge(tokens[index][2 * TB : 2 * TB + 16]) for index in range(PIECES)]
    for pair in range(2):
        at = PAIRS[pair][0]
        keys = own_ref[0:FR, at : at + 256]
        values = own_ref[FR : 2 * FR, at : at + 256]
        grad_k = None
        for index in range(PIECES):
            extra = extras[index]

            def both(base):
                low = base + 2 * pair
                return jnp.concatenate([extra[low : low + 1], extra[low + 1 : low + 2]], axis=1)

            top, inverse, inner = both(0), both(4), both(8)
            first = jnp.concatenate([extra[12:13]] * 2, axis=1)
            last = jnp.concatenate([extra[13:14]] * 2, axis=1)
            block = blocked(tokens[index][TB : 2 * TB], pair)
            cot = blocked(tokens[index][0:TB], pair)
            scores = (
                lax.dot_general(keys, block, NT, preferred_element_type=jnp.float32) * SCALE
            )
            weights = []
            for half in range(2):
                frame = (2 * here + half).astype(jnp.float32)
                allowed = (frame >= first) & (frame < last)
                weights.append(
                    jnp.exp(scores[half * EB : (half + 1) * EB] - jnp.where(allowed, top, jnp.inf))
                )
            probs = jnp.concatenate(weights, axis=0) * inverse
            grads = lax.dot_general(values, cot, NT, preferred_element_type=jnp.float32)
            ds = (probs * (grads - inner)).astype(jnp.bfloat16)
            part_v = jnp.dot(
                probs.astype(jnp.bfloat16), cot, preferred_element_type=jnp.float32
            )
            part_k = jnp.dot(ds, block, preferred_element_type=jnp.float32)
            if grad_k is None:
                grad_k, grad_v = part_k, part_v
            else:
                grad_k, grad_v = grad_k + part_k, grad_v + part_v
        totals.append((grad_k * SCALE, grad_v))
    for which, out in ((0, gk_ref), (1, gv_ref)):
        low, high = totals[0][which], totals[1][which]
        out[:, 0:128] = low[:, :128].astype(out.dtype)
        out[:, 128:256] = (low[:, 128:] + high[:, :128]).astype(out.dtype)
        out[:, 256:384] = high[:, 128:].astype(out.dtype)


VMEM = pl.BlockSpec(memory_space=pltpu.VMEM)
SMEM = pl.BlockSpec(memory_space=pltpu.SMEM)


def call(kernel, outputs, products, scratch=(), scalars=0, vectors=0):
    return pl.pallas_call(
        kernel,
        out_shape=tuple(jax.ShapeDtypeStruct(shape, dtype) for shape, dtype in outputs),
        in_specs=[SMEM] * scalars + [VMEM] * vectors,
        out_specs=(VMEM,) * len(outputs),
        scratch_shapes=[pltpu.VMEM(shape, jnp.float32) for shape in scratch],
        compiler_params=pltpu.CompilerParams(vmem_limit_bytes=24 << 20),
        cost_estimate=pl.CostEstimate(
            flops=products * 2 * 512 * 1280 * 256,
            bytes_accessed=4 << 20,
            transcendentals=512 * 1280,
        ),
    )


def per_device(queries, keys, values, grad_out, gain, band_start, band_end):
    f32, bf16 = jnp.float32, jnp.bfloat16
    here = lax.axis_index("seq")
    core = lax.rem(here, 2)
    own, query, grad, gain_row = pl.pallas_call(
        pack_kernel,
        out_shape=(
            jax.ShapeDtypeStruct((2 * FR, W), bf16),
            jax.ShapeDtypeStruct((TB, W), bf16),
            jax.ShapeDtypeStruct((TB, W), bf16),
            jax.ShapeDtypeStruct((1, W), f32),
        ),
        in_specs=[pl.BlockSpec(memory_space=pltpu.HBM)] * 5,
        out_specs=(VMEM,) * 4,
        scratch_shapes=[pltpu.VMEM((W,), f32), pltpu.SemaphoreType.DMA((5,))],
        compiler_params=pltpu.CompilerParams(vmem_limit_bytes=24 << 20),
        name="pack",
    )(*[
        pltpu.with_memory_space_constraint(array, pltpu.HBM)
        for array in (keys[0], values[0], queries[0], grad_out[0], gain)
    ])
    below = permute(own, "seq", lambda i: i + 2)
    above = permute(own, "seq", lambda i: i - 2)
    partner = permute(own, "seq", lambda i: i ^ 1)
    beyond = permute(jnp.where(core == 0, above, below), "seq", lambda i: i ^ 1)
    pieces = (own, partner, below, above, beyond)
    whole = (2 * TB, PIECES * FR)
    attn, probs, stats, norms = call(
        forward_kernel,
        (((TB, W), f32), ((2, *whole), f32), ((TENSOR, 2, TB), f32), ((8, TB), f32)),
        2,
        scratch=((2, *whole),),
        scalars=2,
        vectors=3 + PIECES,
    )(band_start, band_end, query, grad, gain_row, *pieces)
    stats = lax.all_to_all(stats, "tensor", 0, 0, tiled=False)
    attended, gain_part, grad_queries, sent = call(
        token_kernel,
        (((TB, W), bf16), ((SEQ, 1, W), f32), ((TB, W), bf16), ((2 * TB + 16, W), bf16)),
        2,
        scratch=(whole,),
        scalars=2,
        vectors=7 + PIECES,
    )(band_start, band_end, query, grad, gain_row, attn, probs, norms, stats, *pieces)
    tokens = (
        sent,
        permute(sent, "seq", lambda i: i ^ 1),
        permute(sent, "seq", lambda i: i + 2),
        permute(sent, "seq", lambda i: i - 2),
        permute(sent, "seq", lambda i: i - 1 if i % 2 == 0 else i + 1),
    )
    gain_sum = jnp.sum(lax.all_to_all(gain_part, "seq", 0, 0, tiled=False), axis=(0, 1))
    gain_other = lax.ppermute(gain_sum, "dp", [(0, 1), (1, 0)])
    grad_keys, grad_values = call(
        frame_kernel, (((FR, W), bf16), ((FR, W), bf16)), 4, vectors=1 + PIECES
    )(own, *tokens)
    grad_gain = gain_sum + gain_other
    return (
        attended[None],
        grad_queries[None],
        grad_keys[None],
        grad_values[None],
        grad_gain,
    )


def solution(mesh):
    return jax.shard_map(
        per_device,
        mesh=mesh,
        in_specs=(
            P("dp", "seq", "tensor"),
            P("dp", "seq", "tensor"),
            P("dp", "seq", "tensor"),
            P("dp", "seq", "tensor"),
            P("tensor"),
            P("dp", "seq"),
            P("dp", "seq"),
        ),
        out_specs=(
            P("dp", "seq", "tensor"),
            P("dp", "seq", "tensor"),
            P("dp", "seq", "tensor"),
            P("dp", "seq", "tensor"),
            P("tensor"),
        ),
        check_vma=False,
    )
```

```python
import jax
import jax.numpy as jnp
from jax import lax
from jax.experimental import pallas as pl
from jax.experimental.pallas import tpu as pltpu
from jax.sharding import PartitionSpec as P


D = 3072
HD = 96
TB = 128
EB = 128
FR = 256
W = 384
TENSOR = 8
SEQ = 32
SCALE = HD ** (-0.5)
epsilon = 1e-06

PIECES = 5
EARLY = 3
NT = (((1,), (1,)), ((), ()))
PAIRS = ((0, (0, 96)), (128, (64, 160)))


def permute(array, axis, target):
    size = lax.axis_size(axis)
    pairs = [(i, target(i)) for i in range(size) if 0 <= target(i) < size]
    return lax.ppermute(array, axis, pairs)


def offsets(here):
    core = lax.rem(here, 2)
    toward = 1 - 2 * core
    return (0, toward, -2, 2, -toward)


def blocked(rows, pair):
    first, starts = PAIRS[pair]
    part = rows[:, first : first + 256]
    lane = lax.broadcasted_iota(jnp.int32, part.shape, 1)
    zero = jnp.zeros_like(part)
    return jnp.concatenate(
        [jnp.where((lane >= at) & (lane < at + HD), part, zero) for at in starts], axis=0
    )


def side_by_side(pairs):
    lane = lax.broadcasted_iota(jnp.int32, (TB, 256), 1)
    low = jnp.where(lane < HD, pairs[0][:TB], pairs[0][TB:])
    high = jnp.where(lane < 160, pairs[1][:TB], pairs[1][TB:])
    middle = jnp.where(lane[:, :128] < 64, low[:, 128:], high[:, :128])
    return jnp.concatenate([low[:, :128], middle, high[:, 128:]], axis=1)


def to_rows(columns):
    lane = lax.broadcasted_iota(jnp.int32, (TB, TB), 1)
    tile = jnp.zeros((TB, TB), jnp.float32)
    for index, column in enumerate(columns):
        tile = jnp.where(lane == index, column, tile)
    return tile.T


def split(rows):
    terms = []
    for _ in range(3):
        term = rows.astype(jnp.bfloat16)
        rows = rows - term.astype(jnp.float32)
        terms.append(term)
    return jnp.concatenate(terms, axis=1)


def merge(terms):
    terms = terms.astype(jnp.float32)
    return (terms[:, 0:TB] + terms[:, TB : 2 * TB]) + terms[:, 2 * TB : W]


def pack_kernel(
    k_ref, v_ref, q_ref, go_ref, gain_ref, own_ref, query_ref, grad_ref, row_ref, line, sems
):
    moves = (
        (k_ref, own_ref.at[0:FR]),
        (v_ref, own_ref.at[FR : 2 * FR]),
        (q_ref, query_ref),
        (go_ref, grad_ref),
        (gain_ref, line),
    )
    copies = [
        pltpu.make_async_copy(source, target, sems.at[index])
        for index, (source, target) in enumerate(moves)
    ]
    for copy in copies:
        copy.start()
    for copy in copies:
        copy.wait()
    row_ref[...] = line[...].reshape(1, W)


def forward_kernel(
    start_ref, end_ref, q_ref, go_ref, gain_ref, *rest
):
    pieces = rest[:PIECES]
    attn_ref, probs_ref, stats_ref, norms_ref, scores = rest[PIECES:]
    here = lax.axis_index("seq")
    first = start_ref[0, 0]
    last = end_ref[0, 0]
    rows = q_ref[...]
    results = []
    tops = []
    scales = []
    for pair in range(2):
        at = PAIRS[pair][0]
        block = blocked(rows, pair)
        top = None
        for index, offset in enumerate(offsets(here)):
            frames = 2 * (here + offset)
            product = (
                lax.dot_general(
                    block,
                    pieces[index][0:FR, at : at + 256],
                    NT,
                    preferred_element_type=jnp.float32,
                )
                * SCALE
            )
            for half in range(2):
                allowed = (frames + half >= first) & (frames + half < last)
                bias = jnp.where(allowed, 0.0, -jnp.inf)
                part = product[:, half * EB : (half + 1) * EB] + bias
                scores[pair, :, index * FR + half * EB : index * FR + (half + 1) * EB] = part
                top = part if top is None else jnp.maximum(top, part)
        top = jnp.max(top, axis=1, keepdims=True)
        weights = jnp.exp(scores[pair] - top)
        total = jnp.sum(weights, axis=1, keepdims=True)
        inverse = 1.0 / total
        tops += [top[:TB], top[TB:]]
        scales += [inverse[:TB], inverse[TB:]]
        probs = weights * inverse
        probs_ref[pair] = probs
        probs = probs.astype(jnp.bfloat16)
        acc = None
        for index in range(PIECES):
            part = jnp.dot(
                probs[:, index * FR : (index + 1) * FR],
                pieces[index][FR : 2 * FR, at : at + 256],
                preferred_element_type=jnp.float32,
            )
            acc = part if acc is None else acc + part
        results.append(acc)
    attn = side_by_side(results)
    attn_ref[...] = attn
    scaled = go_ref[...].astype(jnp.float32) * gain_ref[...]
    square = jnp.sum(attn * attn, axis=1, keepdims=True)
    cross = jnp.sum(scaled * attn, axis=1, keepdims=True)
    stats = to_rows([*tops, *scales, square, cross])
    norms_ref[...] = stats[0:8]
    for index in range(TENSOR):
        stats_ref[index] = stats[8:10]


def token_kernel(
    start_ref, end_ref, q_ref, go_ref, gain_ref, attn_ref, probs_ref, norms_ref, stats_ref, *rest
):
    pieces = rest[:PIECES]
    attended_ref, gain_part_ref, gq_ref, sent_ref, grads = rest[PIECES:]
    stats = stats_ref[0]
    for index in range(1, TENSOR):
        stats = stats + stats_ref[index]
    row = lax.broadcasted_iota(jnp.int32, (TB, TB), 0)
    tile = jnp.where(row == 0, stats[0:1], jnp.where(row == 1, stats[1:2], 0.0)).T
    inv = lax.rsqrt(tile[:, 0:1] / D + epsilon)
    mean_cross = inv * tile[:, 1:2] / D
    grad = go_ref[...].astype(jnp.float32)
    gain = gain_ref[...]
    normed = attn_ref[...] * inv
    attended_ref[...] = (normed * gain).astype(jnp.bfloat16)
    gain_part_ref[...] = jnp.broadcast_to(
        jnp.sum(grad * normed, axis=0, keepdims=True)[None], (SEQ, 1, W)
    )
    grad_attn = (inv * (grad * gain - normed * mean_cross)).astype(jnp.bfloat16)
    rows = q_ref[...]
    sent_ref[0:TB] = grad_attn
    sent_ref[TB : 2 * TB] = rows
    grad_q = []
    inners = []
    for pair in range(2):
        at = PAIRS[pair][0]
        cot = blocked(grad_attn, pair)
        inner = None
        for index in range(PIECES):
            span = slice(index * FR, (index + 1) * FR)
            part = lax.dot_general(
                cot,
                pieces[index][FR : 2 * FR, at : at + 256],
                NT,
                preferred_element_type=jnp.float32,
            )
            grads[:, span] = part
            part = probs_ref[pair, :, span] * part
            inner = part if inner is None else inner + part
        inner = jnp.sum(inner, axis=1, keepdims=True)
        inners += [inner[:TB], inner[TB:]]
        acc = None
        for index in range(PIECES):
            span = slice(index * FR, (index + 1) * FR)
            ds = (probs_ref[pair, :, span] * (grads[:, span] - inner)).astype(jnp.bfloat16)
            part = jnp.dot(
                ds, pieces[index][0:FR, at : at + 256], preferred_element_type=jnp.float32
            )
            acc = part if acc is None else acc + part
        grad_q.append(acc)
    gq_ref[...] = (side_by_side(grad_q) * SCALE).astype(jnp.bfloat16)
    band = lax.broadcasted_iota(jnp.int32, (4, TB), 0)
    band = jnp.where(band == 0, start_ref[0, 0], end_ref[0, 0]).astype(jnp.float32)
    sent_ref[2 * TB : 2 * TB + 16] = split(
        jnp.concatenate([norms_ref[...], to_rows(inners)[0:4], band], axis=0)
    )


def frame_sums(own_ref, tokens, sums):
    here = lax.axis_index("seq")
    totals = []
    extras = [merge(token[2 * TB : 2 * TB + 16]) for token in tokens]
    for pair in range(2):
        at = PAIRS[pair][0]
        keys = own_ref[0:FR, at : at + 256]
        values = own_ref[FR : 2 * FR, at : at + 256]
        grad_k, grad_v = sums[pair]
        for index, extra in enumerate(extras):

            def both(base):
                low = base + 2 * pair
                return jnp.concatenate([extra[low : low + 1], extra[low + 1 : low + 2]], axis=1)

            top, inverse, inner = both(0), both(4), both(8)
            first = jnp.concatenate([extra[12:13]] * 2, axis=1)
            last = jnp.concatenate([extra[13:14]] * 2, axis=1)
            block = blocked(tokens[index][TB : 2 * TB], pair)
            cot = blocked(tokens[index][0:TB], pair)
            scores = (
                lax.dot_general(keys, block, NT, preferred_element_type=jnp.float32) * SCALE
            )
            weights = []
            for half in range(2):
                frame = (2 * here + half).astype(jnp.float32)
                allowed = (frame >= first) & (frame < last)
                weights.append(
                    jnp.exp(scores[half * EB : (half + 1) * EB] - jnp.where(allowed, top, jnp.inf))
                )
            probs = jnp.concatenate(weights, axis=0) * inverse
            grads = lax.dot_general(values, cot, NT, preferred_element_type=jnp.float32)
            ds = (probs * (grads - inner)).astype(jnp.bfloat16)
            part_v = jnp.dot(
                probs.astype(jnp.bfloat16), cot, preferred_element_type=jnp.float32
            )
            part_k = jnp.dot(ds, block, preferred_element_type=jnp.float32)
            if grad_k is None:
                grad_k, grad_v = part_k, part_v
            else:
                grad_k, grad_v = grad_k + part_k, grad_v + part_v
        totals.append((grad_k, grad_v))
    return totals


def first_frame_kernel(own_ref, *rest):
    totals = frame_sums(own_ref, rest[:EARLY], [(None, None)] * 2)
    for pair in range(2):
        for which in range(2):
            rest[EARLY][pair, which] = totals[pair][which]


def last_frame_kernel(own_ref, sums_ref, *rest):
    tokens = rest[: PIECES - EARLY]
    outs = rest[PIECES - EARLY :]
    sums = [(sums_ref[pair, 0], sums_ref[pair, 1]) for pair in range(2)]
    totals = frame_sums(own_ref, tokens, sums)
    for which, (out, scale) in enumerate(zip(outs, (SCALE, 1.0))):
        low, high = totals[0][which] * scale, totals[1][which] * scale
        out[:, 0:128] = low[:, :128].astype(out.dtype)
        out[:, 128:256] = (low[:, 128:] + high[:, :128]).astype(out.dtype)
        out[:, 256:384] = high[:, 128:].astype(out.dtype)


VMEM = pl.BlockSpec(memory_space=pltpu.VMEM)
SMEM = pl.BlockSpec(memory_space=pltpu.SMEM)


def call(kernel, outputs, products, scratch=(), scalars=0, vectors=0):
    return pl.pallas_call(
        kernel,
        out_shape=tuple(jax.ShapeDtypeStruct(shape, dtype) for shape, dtype in outputs),
        in_specs=[SMEM] * scalars + [VMEM] * vectors,
        out_specs=(VMEM,) * len(outputs),
        scratch_shapes=[pltpu.VMEM(shape, jnp.float32) for shape in scratch],
        compiler_params=pltpu.CompilerParams(vmem_limit_bytes=24 << 20),
        cost_estimate=pl.CostEstimate(
            flops=products * 2 * 512 * 1280 * 256,
            bytes_accessed=4 << 20,
            transcendentals=512 * 1280,
        ),
    )


def per_device(queries, keys, values, grad_out, gain, band_start, band_end):
    f32, bf16 = jnp.float32, jnp.bfloat16
    here = lax.axis_index("seq")
    core = lax.rem(here, 2)
    own, query, grad, gain_row = pl.pallas_call(
        pack_kernel,
        out_shape=(
            jax.ShapeDtypeStruct((2 * FR, W), bf16),
            jax.ShapeDtypeStruct((TB, W), bf16),
            jax.ShapeDtypeStruct((TB, W), bf16),
            jax.ShapeDtypeStruct((1, W), f32),
        ),
        in_specs=[pl.BlockSpec(memory_space=pltpu.HBM)] * 5,
        out_specs=(VMEM,) * 4,
        scratch_shapes=[pltpu.VMEM((W,), f32), pltpu.SemaphoreType.DMA((5,))],
        compiler_params=pltpu.CompilerParams(vmem_limit_bytes=24 << 20),
        name="pack",
    )(*[
        pltpu.with_memory_space_constraint(array, pltpu.HBM)
        for array in (keys[0], values[0], queries[0], grad_out[0], gain)
    ])
    below = permute(own, "seq", lambda i: i + 2)
    above = permute(own, "seq", lambda i: i - 2)
    partner = permute(own, "seq", lambda i: i ^ 1)
    beyond = permute(jnp.where(core == 0, above, below), "seq", lambda i: i ^ 1)
    pieces = (own, partner, below, above, beyond)
    whole = (2 * TB, PIECES * FR)
    attn, probs, stats, norms = call(
        forward_kernel,
        (((TB, W), f32), ((2, *whole), f32), ((TENSOR, 2, TB), f32), ((8, TB), f32)),
        2,
        scratch=((2, *whole),),
        scalars=2,
        vectors=3 + PIECES,
    )(band_start, band_end, query, grad, gain_row, *pieces)
    stats = lax.all_to_all(stats, "tensor", 0, 0, tiled=False)
    attended, gain_part, grad_queries, sent = call(
        token_kernel,
        (((TB, W), bf16), ((SEQ, 1, W), f32), ((TB, W), bf16), ((2 * TB + 16, W), bf16)),
        2,
        scratch=(whole,),
        scalars=2,
        vectors=7 + PIECES,
    )(band_start, band_end, query, grad, gain_row, attn, probs, norms, stats, *pieces)
    spread = lax.all_to_all(gain_part, "seq", 0, 0, tiled=False)
    gain_sum = jnp.sum(spread, axis=(0, 1))
    tokens = (
        sent,
        permute(sent, "seq", lambda i: i ^ 1),
        permute(sent, "seq", lambda i: i + 2),
        permute(sent, "seq", lambda i: i - 2),
        permute(sent, "seq", lambda i: i - 1 if i % 2 == 0 else i + 1),
    )
    gain_other = lax.ppermute(gain_sum, "dp", [(0, 1), (1, 0)])
    (sums,) = call(
        first_frame_kernel, (((2, 2, FR, 256), f32),), 4, vectors=1 + EARLY
    )(own, *tokens[:EARLY])
    grad_keys, grad_values = call(
        last_frame_kernel, (((FR, W), bf16), ((FR, W), bf16)), 4, vectors=2 + PIECES - EARLY
    )(own, sums, *tokens[EARLY:])
    grad_gain = gain_sum + gain_other
    return (
        attended[None],
        grad_queries[None],
        grad_keys[None],
        grad_values[None],
        grad_gain,
    )


def solution(mesh):
    return jax.shard_map(
        per_device,
        mesh=mesh,
        in_specs=(
            P("dp", "seq", "tensor"),
            P("dp", "seq", "tensor"),
            P("dp", "seq", "tensor"),
            P("dp", "seq", "tensor"),
            P("tensor"),
            P("dp", "seq"),
            P("dp", "seq"),
        ),
        out_specs=(
            P("dp", "seq", "tensor"),
            P("dp", "seq", "tensor"),
            P("dp", "seq", "tensor"),
            P("dp", "seq", "tensor"),
            P("tensor"),
        ),
        check_vma=False,
    )
```

```python
import jax
import jax.numpy as jnp
from jax import lax
from jax.experimental import pallas as pl
from jax.experimental.pallas import tpu as pltpu
from jax.sharding import PartitionSpec as P


D = 3072
HD = 96
TB = 128
EB = 128
FR = 256
W = 384
TENSOR = 8
SEQ = 32
SCALE = HD ** (-0.5)
epsilon = 1e-06

PIECES = 5
NT = (((1,), (1,)), ((), ()))
PAIRS = ((0, (0, 96)), (128, (64, 160)))


def permute(array, axis, target):
    size = lax.axis_size(axis)
    pairs = [(i, target(i)) for i in range(size) if 0 <= target(i) < size]
    return lax.ppermute(array, axis, pairs)


def offsets(here):
    core = lax.rem(here, 2)
    toward = 1 - 2 * core
    return (0, toward, -2, 2, -toward)


def blocked(rows, pair):
    first, starts = PAIRS[pair]
    part = rows[:, first : first + 256]
    lane = lax.broadcasted_iota(jnp.int32, part.shape, 1)
    zero = jnp.zeros_like(part)
    return jnp.concatenate(
        [jnp.where((lane >= at) & (lane < at + HD), part, zero) for at in starts], axis=0
    )


def side_by_side(pairs):
    lane = lax.broadcasted_iota(jnp.int32, (TB, 256), 1)
    low = jnp.where(lane < HD, pairs[0][:TB], pairs[0][TB:])
    high = jnp.where(lane < 160, pairs[1][:TB], pairs[1][TB:])
    middle = jnp.where(lane[:, :128] < 64, low[:, 128:], high[:, :128])
    return jnp.concatenate([low[:, :128], middle, high[:, 128:]], axis=1)


def to_rows(columns):
    lane = lax.broadcasted_iota(jnp.int32, (TB, TB), 1)
    tile = jnp.zeros((TB, TB), jnp.float32)
    for index, column in enumerate(columns):
        tile = jnp.where(lane == index, column, tile)
    return tile.T


def split(rows):
    terms = []
    for _ in range(3):
        term = rows.astype(jnp.bfloat16)
        rows = rows - term.astype(jnp.float32)
        terms.append(term)
    return jnp.concatenate(terms, axis=1)


def merge(terms):
    terms = terms.astype(jnp.float32)
    return (terms[:, 0:TB] + terms[:, TB : 2 * TB]) + terms[:, 2 * TB : W]


def pack_kernel(
    k_ref, v_ref, q_ref, go_ref, gain_ref, own_ref, query_ref, grad_ref, row_ref, line, sems
):
    moves = (
        (k_ref, own_ref.at[0:FR]),
        (v_ref, own_ref.at[FR : 2 * FR]),
        (q_ref, query_ref),
        (go_ref, grad_ref),
        (gain_ref, line),
    )
    copies = [
        pltpu.make_async_copy(source, target, sems.at[index])
        for index, (source, target) in enumerate(moves)
    ]
    for copy in copies:
        copy.start()
    for copy in copies:
        copy.wait()
    row_ref[...] = line[...].reshape(1, W)


def forward_kernel(
    start_ref, end_ref, q_ref, go_ref, gain_ref, *rest
):
    pieces = rest[:PIECES]
    attn_ref, probs_ref, stats_ref, norms_ref, scores = rest[PIECES:]
    here = lax.axis_index("seq")
    first = start_ref[0, 0]
    last = end_ref[0, 0]
    rows = q_ref[...]
    results = []
    tops = []
    scales = []
    for pair in range(2):
        at = PAIRS[pair][0]
        block = blocked(rows, pair)
        top = None
        for index, offset in enumerate(offsets(here)):
            frames = 2 * (here + offset)
            product = (
                lax.dot_general(
                    block,
                    pieces[index][0:FR, at : at + 256],
                    NT,
                    preferred_element_type=jnp.float32,
                )
                * SCALE
            )
            for half in range(2):
                allowed = (frames + half >= first) & (frames + half < last)
                bias = jnp.where(allowed, 0.0, -jnp.inf)
                part = product[:, half * EB : (half + 1) * EB] + bias
                scores[pair, :, index * FR + half * EB : index * FR + (half + 1) * EB] = part
                top = part if top is None else jnp.maximum(top, part)
        top = jnp.max(top, axis=1, keepdims=True)
        weights = jnp.exp(scores[pair] - top)
        total = jnp.sum(weights, axis=1, keepdims=True)
        inverse = 1.0 / total
        tops += [top[:TB], top[TB:]]
        scales += [inverse[:TB], inverse[TB:]]
        probs = weights * inverse
        probs_ref[pair] = probs
        probs = probs.astype(jnp.bfloat16)
        acc = None
        for index in range(PIECES):
            part = jnp.dot(
                probs[:, index * FR : (index + 1) * FR],
                pieces[index][FR : 2 * FR, at : at + 256],
                preferred_element_type=jnp.float32,
            )
            acc = part if acc is None else acc + part
        results.append(acc)
    attn = side_by_side(results)
    attn_ref[...] = attn
    scaled = go_ref[...].astype(jnp.float32) * gain_ref[...]
    square = jnp.sum(attn * attn, axis=1, keepdims=True)
    cross = jnp.sum(scaled * attn, axis=1, keepdims=True)
    stats = to_rows([*tops, *scales, square, cross])
    norms_ref[...] = stats[0:8]
    for index in range(TENSOR):
        stats_ref[index] = stats[8:10]


def norm_kernel(go_ref, gain_ref, attn_ref, stats_ref, attended_ref, gain_part_ref, cot_ref):
    stats = stats_ref[0]
    for index in range(1, TENSOR):
        stats = stats + stats_ref[index]
    row = lax.broadcasted_iota(jnp.int32, (TB, TB), 0)
    tile = jnp.where(row == 0, stats[0:1], jnp.where(row == 1, stats[1:2], 0.0)).T
    inv = lax.rsqrt(tile[:, 0:1] / D + epsilon)
    mean_cross = inv * tile[:, 1:2] / D
    grad = go_ref[...].astype(jnp.float32)
    gain = gain_ref[...]
    normed = attn_ref[...] * inv
    attended_ref[...] = (normed * gain).astype(jnp.bfloat16)
    gain_part_ref[...] = jnp.sum(grad * normed, axis=0, keepdims=True)
    cot_ref[...] = (inv * (grad * gain - normed * mean_cross)).astype(jnp.bfloat16)


def token_kernel(start_ref, end_ref, q_ref, cot_ref, probs_ref, norms_ref, *rest):
    pieces = rest[:PIECES]
    gq_ref, sent_ref, grads = rest[PIECES:]
    grad_attn = cot_ref[...]
    sent_ref[0:TB] = grad_attn
    sent_ref[TB : 2 * TB] = q_ref[...]
    grad_q = []
    inners = []
    for pair in range(2):
        at = PAIRS[pair][0]
        cot = blocked(grad_attn, pair)
        inner = None
        for index in range(PIECES):
            span = slice(index * FR, (index + 1) * FR)
            part = lax.dot_general(
                cot,
                pieces[index][FR : 2 * FR, at : at + 256],
                NT,
                preferred_element_type=jnp.float32,
            )
            grads[:, span] = part
            part = probs_ref[pair, :, span] * part
            inner = part if inner is None else inner + part
        inner = jnp.sum(inner, axis=1, keepdims=True)
        inners += [inner[:TB], inner[TB:]]
        acc = None
        for index in range(PIECES):
            span = slice(index * FR, (index + 1) * FR)
            ds = (probs_ref[pair, :, span] * (grads[:, span] - inner)).astype(jnp.bfloat16)
            part = jnp.dot(
                ds, pieces[index][0:FR, at : at + 256], preferred_element_type=jnp.float32
            )
            acc = part if acc is None else acc + part
        grad_q.append(acc)
    gq_ref[...] = (side_by_side(grad_q) * SCALE).astype(jnp.bfloat16)
    band = lax.broadcasted_iota(jnp.int32, (4, TB), 0)
    band = jnp.where(band == 0, start_ref[0, 0], end_ref[0, 0]).astype(jnp.float32)
    sent_ref[2 * TB : 2 * TB + 16] = split(
        jnp.concatenate([norms_ref[...], to_rows(inners)[0:4], band], axis=0)
    )


def spread_kernel(mine_ref, other_ref, out_ref):
    out_ref[...] = jnp.broadcast_to((mine_ref[...] + other_ref[...])[None], (SEQ, 1, W))


def frame_sums(own_ref, tokens):
    here = lax.axis_index("seq")
    totals = []
    extras = [merge(token[2 * TB : 2 * TB + 16]) for token in tokens]
    for pair in range(2):
        at = PAIRS[pair][0]
        keys = own_ref[0:FR, at : at + 256]
        values = own_ref[FR : 2 * FR, at : at + 256]
        grad_k = grad_v = None
        for index, extra in enumerate(extras):

            def both(base):
                low = base + 2 * pair
                return jnp.concatenate([extra[low : low + 1], extra[low + 1 : low + 2]], axis=1)

            top, inverse, inner = both(0), both(4), both(8)
            first = jnp.concatenate([extra[12:13]] * 2, axis=1)
            last = jnp.concatenate([extra[13:14]] * 2, axis=1)
            block = blocked(tokens[index][TB : 2 * TB], pair)
            cot = blocked(tokens[index][0:TB], pair)
            scores = (
                lax.dot_general(keys, block, NT, preferred_element_type=jnp.float32) * SCALE
            )
            weights = []
            for half in range(2):
                frame = (2 * here + half).astype(jnp.float32)
                allowed = (frame >= first) & (frame < last)
                weights.append(
                    jnp.exp(scores[half * EB : (half + 1) * EB] - jnp.where(allowed, top, jnp.inf))
                )
            probs = jnp.concatenate(weights, axis=0) * inverse
            grads = lax.dot_general(values, cot, NT, preferred_element_type=jnp.float32)
            ds = (probs * (grads - inner)).astype(jnp.bfloat16)
            part_v = jnp.dot(
                probs.astype(jnp.bfloat16), cot, preferred_element_type=jnp.float32
            )
            part_k = jnp.dot(ds, block, preferred_element_type=jnp.float32)
            if grad_k is None:
                grad_k, grad_v = part_k, part_v
            else:
                grad_k, grad_v = grad_k + part_k, grad_v + part_v
        totals.append((grad_k, grad_v))
    return totals


def frame_kernel(own_ref, *rest):
    tokens = rest[:PIECES]
    outs = rest[PIECES:]
    totals = frame_sums(own_ref, tokens)
    for which, (out, scale) in enumerate(zip(outs, (SCALE, 1.0))):
        low, high = totals[0][which] * scale, totals[1][which] * scale
        out[:, 0:128] = low[:, :128].astype(out.dtype)
        out[:, 128:256] = (low[:, 128:] + high[:, :128]).astype(out.dtype)
        out[:, 256:384] = high[:, 128:].astype(out.dtype)


VMEM = pl.BlockSpec(memory_space=pltpu.VMEM)
SMEM = pl.BlockSpec(memory_space=pltpu.SMEM)


def call(kernel, outputs, products, scratch=(), scalars=0, vectors=0):
    return pl.pallas_call(
        kernel,
        out_shape=tuple(jax.ShapeDtypeStruct(shape, dtype) for shape, dtype in outputs),
        in_specs=[SMEM] * scalars + [VMEM] * vectors,
        out_specs=(VMEM,) * len(outputs),
        scratch_shapes=[pltpu.VMEM(shape, jnp.float32) for shape in scratch],
        compiler_params=pltpu.CompilerParams(vmem_limit_bytes=24 << 20),
        cost_estimate=pl.CostEstimate(
            flops=products * 2 * 512 * 1280 * 256,
            bytes_accessed=4 << 20,
            transcendentals=512 * 1280,
        ),
    )


def per_device(queries, keys, values, grad_out, gain, band_start, band_end):
    f32, bf16 = jnp.float32, jnp.bfloat16
    here = lax.axis_index("seq")
    core = lax.rem(here, 2)
    own, query, grad, gain_row = pl.pallas_call(
        pack_kernel,
        out_shape=(
            jax.ShapeDtypeStruct((2 * FR, W), bf16),
            jax.ShapeDtypeStruct((TB, W), bf16),
            jax.ShapeDtypeStruct((TB, W), bf16),
            jax.ShapeDtypeStruct((1, W), f32),
        ),
        in_specs=[pl.BlockSpec(memory_space=pltpu.HBM)] * 5,
        out_specs=(VMEM,) * 4,
        scratch_shapes=[pltpu.VMEM((W,), f32), pltpu.SemaphoreType.DMA((5,))],
        compiler_params=pltpu.CompilerParams(vmem_limit_bytes=24 << 20),
        name="pack",
    )(*[
        pltpu.with_memory_space_constraint(array, pltpu.HBM)
        for array in (keys[0], values[0], queries[0], grad_out[0], gain)
    ])
    below = permute(own, "seq", lambda i: i + 2)
    above = permute(own, "seq", lambda i: i - 2)
    partner = permute(own, "seq", lambda i: i ^ 1)
    beyond = permute(jnp.where(core == 0, above, below), "seq", lambda i: i ^ 1)
    pieces = (own, partner, below, above, beyond)
    whole = (2 * TB, PIECES * FR)
    attn, probs, stats, norms = call(
        forward_kernel,
        (((TB, W), f32), ((2, *whole), f32), ((TENSOR, 2, TB), f32), ((8, TB), f32)),
        2,
        scratch=((2, *whole),),
        scalars=2,
        vectors=3 + PIECES,
    )(band_start, band_end, query, grad, gain_row, *pieces)
    stats = lax.all_to_all(stats, "tensor", 0, 0, tiled=False)
    attended, gain_part, cot = call(
        norm_kernel, (((TB, W), bf16), ((1, W), f32), ((TB, W), bf16)), 0, vectors=4
    )(grad, gain_row, attn, stats)
    gain_other = lax.ppermute(gain_part, "dp", [(0, 1), (1, 0)])
    grad_queries, sent = call(
        token_kernel,
        (((TB, W), bf16), ((2 * TB + 16, W), bf16)),
        2,
        scratch=(whole,),
        scalars=2,
        vectors=4 + PIECES,
    )(band_start, band_end, query, cot, probs, norms, *pieces)
    (gain_both,) = call(spread_kernel, (((SEQ, 1, W), f32),), 0, vectors=2)(gain_part, gain_other)
    spread = lax.all_to_all(gain_both, "seq", 0, 0, tiled=False)
    tokens = (
        sent,
        permute(sent, "seq", lambda i: i ^ 1),
        permute(sent, "seq", lambda i: i + 2),
        permute(sent, "seq", lambda i: i - 2),
        permute(sent, "seq", lambda i: i - 1 if i % 2 == 0 else i + 1),
    )
    grad_keys, grad_values = call(
        frame_kernel, (((FR, W), bf16), ((FR, W), bf16)), 4, vectors=1 + PIECES
    )(own, *tokens)
    grad_gain = jnp.sum(spread, axis=(0, 1))
    return (
        attended[None],
        grad_queries[None],
        grad_keys[None],
        grad_values[None],
        grad_gain,
    )


def solution(mesh):
    return jax.shard_map(
        per_device,
        mesh=mesh,
        in_specs=(
            P("dp", "seq", "tensor"),
            P("dp", "seq", "tensor"),
            P("dp", "seq", "tensor"),
            P("dp", "seq", "tensor"),
            P("tensor"),
            P("dp", "seq"),
            P("dp", "seq"),
        ),
        out_specs=(
            P("dp", "seq", "tensor"),
            P("dp", "seq", "tensor"),
            P("dp", "seq", "tensor"),
            P("dp", "seq", "tensor"),
            P("tensor"),
        ),
        check_vma=False,
    )
```

```python
import jax
import jax.numpy as jnp
from jax import lax
from jax.experimental import pallas as pl
from jax.experimental.pallas import tpu as pltpu
from jax.sharding import PartitionSpec as P


D = 3072
HD = 96
TB = 128
EB = 128
FR = 256
W = 384
TENSOR = 8
SEQ = 32
SCALE = HD ** (-0.5)
epsilon = 1e-06

PIECES = 5
NT = (((1,), (1,)), ((), ()))
PAIRS = ((0, (0, 96)), (128, (64, 160)))


def permute(array, axis, target):
    size = lax.axis_size(axis)
    pairs = [(i, target(i)) for i in range(size) if 0 <= target(i) < size]
    return lax.ppermute(array, axis, pairs)


def offsets(here):
    core = lax.rem(here, 2)
    toward = 1 - 2 * core
    return (0, toward, -2, 2, -toward)


def blocked(rows, pair):
    first, starts = PAIRS[pair]
    part = rows[:, first : first + 256]
    lane = lax.broadcasted_iota(jnp.int32, part.shape, 1)
    zero = jnp.zeros_like(part)
    return jnp.concatenate(
        [jnp.where((lane >= at) & (lane < at + HD), part, zero) for at in starts], axis=0
    )


def side_by_side(pairs):
    lane = lax.broadcasted_iota(jnp.int32, (TB, 256), 1)
    low = jnp.where(lane < HD, pairs[0][:TB], pairs[0][TB:])
    high = jnp.where(lane < 160, pairs[1][:TB], pairs[1][TB:])
    middle = jnp.where(lane[:, :128] < 64, low[:, 128:], high[:, :128])
    return jnp.concatenate([low[:, :128], middle, high[:, 128:]], axis=1)


def to_rows(columns):
    lane = lax.broadcasted_iota(jnp.int32, (TB, TB), 1)
    tile = jnp.zeros((TB, TB), jnp.float32)
    for index, column in enumerate(columns):
        tile = jnp.where(lane == index, column, tile)
    return tile.T


def split(rows):
    terms = []
    for _ in range(3):
        term = rows.astype(jnp.bfloat16)
        rows = rows - term.astype(jnp.float32)
        terms.append(term)
    return jnp.concatenate(terms, axis=1)


def merge(terms):
    terms = terms.astype(jnp.float32)
    return (terms[:, 0:TB] + terms[:, TB : 2 * TB]) + terms[:, 2 * TB : W]


def pack_kernel(
    k_ref, v_ref, q_ref, go_ref, gain_ref, own_ref, query_ref, grad_ref, row_ref, line, sems
):
    moves = (
        (k_ref, own_ref.at[0:FR]),
        (v_ref, own_ref.at[FR : 2 * FR]),
        (q_ref, query_ref),
        (go_ref, grad_ref),
        (gain_ref, line),
    )
    copies = [
        pltpu.make_async_copy(source, target, sems.at[index])
        for index, (source, target) in enumerate(moves)
    ]
    for copy in copies:
        copy.start()
    for copy in copies:
        copy.wait()
    row_ref[...] = line[...].reshape(1, W)


def forward_kernel(
    start_ref, end_ref, q_ref, go_ref, gain_ref, *rest
):
    pieces = rest[:PIECES]
    attn_ref, probs_ref, stats_ref, norms_ref, scores = rest[PIECES:]
    here = lax.axis_index("seq")
    first = start_ref[0, 0]
    last = end_ref[0, 0]
    rows = q_ref[...]
    results = []
    tops = []
    scales = []
    for pair in range(2):
        at = PAIRS[pair][0]
        block = blocked(rows, pair)
        top = None
        for index, offset in enumerate(offsets(here)):
            frames = 2 * (here + offset)
            product = (
                lax.dot_general(
                    block,
                    pieces[index][0:FR, at : at + 256],
                    NT,
                    preferred_element_type=jnp.float32,
                )
                * SCALE
            )
            for half in range(2):
                allowed = (frames + half >= first) & (frames + half < last)
                bias = jnp.where(allowed, 0.0, -jnp.inf)
                part = product[:, half * EB : (half + 1) * EB] + bias
                scores[pair, :, index * FR + half * EB : index * FR + (half + 1) * EB] = part
                top = part if top is None else jnp.maximum(top, part)
        top = jnp.max(top, axis=1, keepdims=True)
        weights = jnp.exp(scores[pair] - top)
        total = jnp.sum(weights, axis=1, keepdims=True)
        inverse = 1.0 / total
        tops += [top[:TB], top[TB:]]
        scales += [inverse[:TB], inverse[TB:]]
        probs = weights * inverse
        probs_ref[pair] = probs
        probs = probs.astype(jnp.bfloat16)
        acc = None
        for index in range(PIECES):
            part = jnp.dot(
                probs[:, index * FR : (index + 1) * FR],
                pieces[index][FR : 2 * FR, at : at + 256],
                preferred_element_type=jnp.float32,
            )
            acc = part if acc is None else acc + part
        results.append(acc)
    attn = side_by_side(results)
    attn_ref[...] = attn
    scaled = go_ref[...].astype(jnp.float32) * gain_ref[...]
    square = jnp.sum(attn * attn, axis=1, keepdims=True)
    cross = jnp.sum(scaled * attn, axis=1, keepdims=True)
    stats = to_rows([*tops, *scales, square, cross])
    norms_ref[...] = stats[0:8]
    for index in range(TENSOR):
        stats_ref[index] = stats[8:10]


def token_kernel(
    start_ref, end_ref, q_ref, go_ref, gain_ref, attn_ref, probs_ref, norms_ref, stats_ref, *rest
):
    pieces = rest[:PIECES]
    attended_ref, gain_part_ref, gq_ref, sent_ref, grads = rest[PIECES:]
    stats = stats_ref[0]
    for index in range(1, TENSOR):
        stats = stats + stats_ref[index]
    row = lax.broadcasted_iota(jnp.int32, (TB, TB), 0)
    tile = jnp.where(row == 0, stats[0:1], jnp.where(row == 1, stats[1:2], 0.0)).T
    inv = lax.rsqrt(tile[:, 0:1] / D + epsilon)
    mean_cross = inv * tile[:, 1:2] / D
    grad = go_ref[...].astype(jnp.float32)
    gain = gain_ref[...]
    normed = attn_ref[...] * inv
    attended_ref[...] = (normed * gain).astype(jnp.bfloat16)
    gain_part_ref[...] = jnp.broadcast_to(
        jnp.sum(grad * normed, axis=0, keepdims=True)[None], (SEQ, 1, W)
    )
    grad_attn = (inv * (grad * gain - normed * mean_cross)).astype(jnp.bfloat16)
    rows = q_ref[...]
    sent_ref[0:TB] = grad_attn
    sent_ref[TB : 2 * TB] = rows
    grad_q = []
    inners = []
    for pair in range(2):
        at = PAIRS[pair][0]
        cot = blocked(grad_attn, pair)
        inner = None
        for index in range(PIECES):
            span = slice(index * FR, (index + 1) * FR)
            part = lax.dot_general(
                cot,
                pieces[index][FR : 2 * FR, at : at + 256],
                NT,
                preferred_element_type=jnp.float32,
            )
            grads[:, span] = part
            part = probs_ref[pair, :, span] * part
            inner = part if inner is None else inner + part
        inner = jnp.sum(inner, axis=1, keepdims=True)
        inners += [inner[:TB], inner[TB:]]
        acc = None
        for index in range(PIECES):
            span = slice(index * FR, (index + 1) * FR)
            ds = (probs_ref[pair, :, span] * (grads[:, span] - inner)).astype(jnp.bfloat16)
            part = jnp.dot(
                ds, pieces[index][0:FR, at : at + 256], preferred_element_type=jnp.float32
            )
            acc = part if acc is None else acc + part
        grad_q.append(acc)
    gq_ref[...] = (side_by_side(grad_q) * SCALE).astype(jnp.bfloat16)
    band = lax.broadcasted_iota(jnp.int32, (4, TB), 0)
    band = jnp.where(band == 0, start_ref[0, 0], end_ref[0, 0]).astype(jnp.float32)
    sent_ref[2 * TB : 2 * TB + 16] = split(
        jnp.concatenate([norms_ref[...], to_rows(inners)[0:4], band], axis=0)
    )


def frame_sums(kv_ref, here, tokens):
    totals = []
    extras = [merge(token[2 * TB : 2 * TB + 16]) for token in tokens]
    for pair in range(2):
        at = PAIRS[pair][0]
        keys = kv_ref[0:FR, at : at + 256]
        values = kv_ref[FR : 2 * FR, at : at + 256]
        grad_k = grad_v = None
        for index, extra in enumerate(extras):

            def both(base):
                low = base + 2 * pair
                return jnp.concatenate([extra[low : low + 1], extra[low + 1 : low + 2]], axis=1)

            top, inverse, inner = both(0), both(4), both(8)
            first = jnp.concatenate([extra[12:13]] * 2, axis=1)
            last = jnp.concatenate([extra[13:14]] * 2, axis=1)
            block = blocked(tokens[index][TB : 2 * TB], pair)
            cot = blocked(tokens[index][0:TB], pair)
            scores = (
                lax.dot_general(keys, block, NT, preferred_element_type=jnp.float32) * SCALE
            )
            weights = []
            for half in range(2):
                frame = (2 * here + half).astype(jnp.float32)
                allowed = (frame >= first) & (frame < last)
                weights.append(
                    jnp.exp(scores[half * EB : (half + 1) * EB] - jnp.where(allowed, top, jnp.inf))
                )
            probs = jnp.concatenate(weights, axis=0) * inverse
            grads = lax.dot_general(values, cot, NT, preferred_element_type=jnp.float32)
            ds = (probs * (grads - inner)).astype(jnp.bfloat16)
            part_v = jnp.dot(
                probs.astype(jnp.bfloat16), cot, preferred_element_type=jnp.float32
            )
            part_k = jnp.dot(ds, block, preferred_element_type=jnp.float32)
            if grad_k is None:
                grad_k, grad_v = part_k, part_v
            else:
                grad_k, grad_v = grad_k + part_k, grad_v + part_v
        totals.append((grad_k, grad_v))
    return totals


def columns(totals, which):
    low, high = totals[0][which], totals[1][which]
    return ((0, low[:, :128]), (128, low[:, 128:] + high[:, :128]), (256, high[:, 128:]))


def partner_frame_kernel(kv_ref, sent_ref, below_ref, above_ref, out_ref):
    here = lax.axis_index("seq")
    core = lax.rem(here, 2)
    far = jnp.where(core == 0, above_ref[...], below_ref[...])
    totals = frame_sums(kv_ref, here + 1 - 2 * core, (sent_ref[...], far))
    for which in range(2):
        for at, part in columns(totals, which):
            out_ref[which * FR : (which + 1) * FR, at : at + 128] = part.astype(out_ref.dtype)


def own_frame_kernel(kv_ref, sent_ref, below_ref, above_ref, more_ref, gk_ref, gv_ref):
    tokens = (sent_ref[...], below_ref[...], above_ref[...])
    totals = frame_sums(kv_ref, lax.axis_index("seq"), tokens)
    for which, (out, scale) in enumerate(((gk_ref, SCALE), (gv_ref, 1.0))):
        for at, part in columns(totals, which):
            more = more_ref[which * FR : (which + 1) * FR, at : at + 128].astype(jnp.float32)
            out[:, at : at + 128] = ((part + more) * scale).astype(out.dtype)


VMEM = pl.BlockSpec(memory_space=pltpu.VMEM)
SMEM = pl.BlockSpec(memory_space=pltpu.SMEM)


def call(kernel, outputs, products, scratch=(), scalars=0, vectors=0):
    return pl.pallas_call(
        kernel,
        out_shape=tuple(jax.ShapeDtypeStruct(shape, dtype) for shape, dtype in outputs),
        in_specs=[SMEM] * scalars + [VMEM] * vectors,
        out_specs=(VMEM,) * len(outputs),
        scratch_shapes=[pltpu.VMEM(shape, jnp.float32) for shape in scratch],
        compiler_params=pltpu.CompilerParams(vmem_limit_bytes=24 << 20),
        cost_estimate=pl.CostEstimate(
            flops=products * 2 * 512 * 1280 * 256,
            bytes_accessed=4 << 20,
            transcendentals=512 * 1280,
        ),
    )


def per_device(queries, keys, values, grad_out, gain, band_start, band_end):
    f32, bf16 = jnp.float32, jnp.bfloat16
    here = lax.axis_index("seq")
    core = lax.rem(here, 2)
    own, query, grad, gain_row = pl.pallas_call(
        pack_kernel,
        out_shape=(
            jax.ShapeDtypeStruct((2 * FR, W), bf16),
            jax.ShapeDtypeStruct((TB, W), bf16),
            jax.ShapeDtypeStruct((TB, W), bf16),
            jax.ShapeDtypeStruct((1, W), f32),
        ),
        in_specs=[pl.BlockSpec(memory_space=pltpu.HBM)] * 5,
        out_specs=(VMEM,) * 4,
        scratch_shapes=[pltpu.VMEM((W,), f32), pltpu.SemaphoreType.DMA((5,))],
        compiler_params=pltpu.CompilerParams(vmem_limit_bytes=24 << 20),
        name="pack",
    )(*[
        pltpu.with_memory_space_constraint(array, pltpu.HBM)
        for array in (keys[0], values[0], queries[0], grad_out[0], gain)
    ])
    below = permute(own, "seq", lambda i: i + 2)
    above = permute(own, "seq", lambda i: i - 2)
    partner = permute(own, "seq", lambda i: i ^ 1)
    beyond = permute(jnp.where(core == 0, above, below), "seq", lambda i: i ^ 1)
    pieces = (own, partner, below, above, beyond)
    whole = (2 * TB, PIECES * FR)
    attn, probs, stats, norms = call(
        forward_kernel,
        (((TB, W), f32), ((2, *whole), f32), ((TENSOR, 2, TB), f32), ((8, TB), f32)),
        2,
        scratch=((2, *whole),),
        scalars=2,
        vectors=3 + PIECES,
    )(band_start, band_end, query, grad, gain_row, *pieces)
    stats = lax.all_to_all(stats, "tensor", 0, 0, tiled=False)
    attended, gain_part, grad_queries, sent = call(
        token_kernel,
        (((TB, W), bf16), ((SEQ, 1, W), f32), ((TB, W), bf16), ((2 * TB + 16, W), bf16)),
        2,
        scratch=(whole,),
        scalars=2,
        vectors=7 + PIECES,
    )(band_start, band_end, query, grad, gain_row, attn, probs, norms, stats, *pieces)
    spread = lax.all_to_all(gain_part, "seq", 0, 0, tiled=False)
    gain_sum = jnp.sum(spread, axis=(0, 1))
    tokens = (sent, permute(sent, "seq", lambda i: i + 2), permute(sent, "seq", lambda i: i - 2))
    (to_partner,) = call(
        partner_frame_kernel, (((2 * FR, W), bf16),), 2, vectors=4
    )(partner, *tokens)
    from_partner = permute(to_partner, "seq", lambda i: i ^ 1)
    gain_other = lax.ppermute(gain_sum, "dp", [(0, 1), (1, 0)])
    grad_keys, grad_values = call(
        own_frame_kernel, (((FR, W), bf16), ((FR, W), bf16)), 2, vectors=5
    )(own, *tokens, from_partner)
    grad_gain = gain_sum + gain_other
    return (
        attended[None],
        grad_queries[None],
        grad_keys[None],
        grad_values[None],
        grad_gain,
    )


def solution(mesh):
    return jax.shard_map(
        per_device,
        mesh=mesh,
        in_specs=(
            P("dp", "seq", "tensor"),
            P("dp", "seq", "tensor"),
            P("dp", "seq", "tensor"),
            P("dp", "seq", "tensor"),
            P("tensor"),
            P("dp", "seq"),
            P("dp", "seq"),
        ),
        out_specs=(
            P("dp", "seq", "tensor"),
            P("dp", "seq", "tensor"),
            P("dp", "seq", "tensor"),
            P("dp", "seq", "tensor"),
            P("tensor"),
        ),
        check_vma=False,
    )
```

```python
import jax
import jax.numpy as jnp
from jax import lax
from jax.experimental import pallas as pl
from jax.experimental.pallas import tpu as pltpu
from jax.sharding import PartitionSpec as P


D = 3072
HD = 96
TB = 128
EB = 128
FR = 256
W = 384
TENSOR = 8
SEQ = 32
SCALE = HD ** (-0.5)
epsilon = 1e-06

PIECES = 5
NT = (((1,), (1,)), ((), ()))
PAIRS = ((0, (0, 96)), (128, (64, 160)))


def permute(array, axis, target):
    size = lax.axis_size(axis)
    pairs = [(i, target(i)) for i in range(size) if 0 <= target(i) < size]
    return lax.ppermute(array, axis, pairs)


def offsets(here):
    core = lax.rem(here, 2)
    toward = 1 - 2 * core
    return (0, toward, -2, 2, -toward)


def blocked(rows, pair):
    first, starts = PAIRS[pair]
    part = rows[:, first : first + 256]
    lane = lax.broadcasted_iota(jnp.int32, part.shape, 1)
    zero = jnp.zeros_like(part)
    return jnp.concatenate(
        [jnp.where((lane >= at) & (lane < at + HD), part, zero) for at in starts], axis=0
    )


def side_by_side(pairs):
    lane = lax.broadcasted_iota(jnp.int32, (TB, 256), 1)
    low = jnp.where(lane < HD, pairs[0][:TB], pairs[0][TB:])
    high = jnp.where(lane < 160, pairs[1][:TB], pairs[1][TB:])
    middle = jnp.where(lane[:, :128] < 64, low[:, 128:], high[:, :128])
    return jnp.concatenate([low[:, :128], middle, high[:, 128:]], axis=1)


def to_rows(columns):
    lane = lax.broadcasted_iota(jnp.int32, (TB, TB), 1)
    tile = jnp.zeros((TB, TB), jnp.float32)
    for index, column in enumerate(columns):
        tile = jnp.where(lane == index, column, tile)
    return tile.T


def split(rows):
    terms = []
    for _ in range(3):
        term = rows.astype(jnp.bfloat16)
        rows = rows - term.astype(jnp.float32)
        terms.append(term)
    return jnp.concatenate(terms, axis=1)


def merge(terms):
    terms = terms.astype(jnp.float32)
    return (terms[:, 0:TB] + terms[:, TB : 2 * TB]) + terms[:, 2 * TB : W]


def pack_kernel(
    k_ref, v_ref, q_ref, go_ref, gain_ref, own_ref, query_ref, grad_ref, row_ref, line, sems
):
    moves = (
        (k_ref, own_ref.at[0:FR]),
        (v_ref, own_ref.at[FR : 2 * FR]),
        (q_ref, query_ref),
        (go_ref, grad_ref),
        (gain_ref, line),
    )
    copies = [
        pltpu.make_async_copy(source, target, sems.at[index])
        for index, (source, target) in enumerate(moves)
    ]
    for copy in copies:
        copy.start()
    for copy in copies:
        copy.wait()
    row_ref[...] = line[...].reshape(1, W)


def forward_kernel(
    start_ref, end_ref, q_ref, go_ref, gain_ref, *rest
):
    pieces = rest[:PIECES]
    attn_ref, probs_ref, stats_ref, norms_ref, scores = rest[PIECES:]
    here = lax.axis_index("seq")
    first = start_ref[0, 0]
    last = end_ref[0, 0]
    rows = q_ref[...]
    results = []
    tops = []
    scales = []
    for pair in range(2):
        at = PAIRS[pair][0]
        block = blocked(rows, pair)
        top = None
        for index, offset in enumerate(offsets(here)):
            frames = 2 * (here + offset)
            product = (
                lax.dot_general(
                    block,
                    pieces[index][0:FR, at : at + 256],
                    NT,
                    preferred_element_type=jnp.float32,
                )
                * SCALE
            )
            for half in range(2):
                allowed = (frames + half >= first) & (frames + half < last)
                bias = jnp.where(allowed, 0.0, -jnp.inf)
                part = product[:, half * EB : (half + 1) * EB] + bias
                scores[pair, :, index * FR + half * EB : index * FR + (half + 1) * EB] = part
                top = part if top is None else jnp.maximum(top, part)
        top = jnp.max(top, axis=1, keepdims=True)
        weights = jnp.exp(scores[pair] - top)
        total = jnp.sum(weights, axis=1, keepdims=True)
        inverse = 1.0 / total
        tops += [top[:TB], top[TB:]]
        scales += [inverse[:TB], inverse[TB:]]
        probs = weights * inverse
        probs_ref[pair] = probs
        probs = probs.astype(jnp.bfloat16)
        acc = None
        for index in range(PIECES):
            part = jnp.dot(
                probs[:, index * FR : (index + 1) * FR],
                pieces[index][FR : 2 * FR, at : at + 256],
                preferred_element_type=jnp.float32,
            )
            acc = part if acc is None else acc + part
        results.append(acc)
    attn = side_by_side(results)
    attn_ref[...] = attn
    scaled = go_ref[...].astype(jnp.float32) * gain_ref[...]
    square = jnp.sum(attn * attn, axis=1, keepdims=True)
    cross = jnp.sum(scaled * attn, axis=1, keepdims=True)
    stats = to_rows([*tops, *scales, square, cross])
    norms_ref[...] = stats[0:8]
    for index in range(TENSOR):
        stats_ref[index] = stats[8:10]


def token_kernel(
    start_ref, end_ref, q_ref, go_ref, gain_ref, attn_ref, probs_ref, norms_ref, stats_ref, *rest
):
    pieces = rest[:PIECES]
    attended_ref, gain_part_ref, gq_ref, sent_ref, grads = rest[PIECES:]
    stats = stats_ref[0]
    for index in range(1, TENSOR):
        stats = stats + stats_ref[index]
    row = lax.broadcasted_iota(jnp.int32, (TB, TB), 0)
    tile = jnp.where(row == 0, stats[0:1], jnp.where(row == 1, stats[1:2], 0.0)).T
    inv = lax.rsqrt(tile[:, 0:1] / D + epsilon)
    mean_cross = inv * tile[:, 1:2] / D
    grad = go_ref[...].astype(jnp.float32)
    gain = gain_ref[...]
    normed = attn_ref[...] * inv
    attended_ref[...] = (normed * gain).astype(jnp.bfloat16)
    gain_part_ref[...] = jnp.sum(grad * normed, axis=0, keepdims=True)
    grad_attn = (inv * (grad * gain - normed * mean_cross)).astype(jnp.bfloat16)
    rows = q_ref[...]
    sent_ref[0:TB] = grad_attn
    sent_ref[TB : 2 * TB] = rows
    grad_q = []
    inners = []
    for pair in range(2):
        at = PAIRS[pair][0]
        cot = blocked(grad_attn, pair)
        inner = None
        for index in range(PIECES):
            span = slice(index * FR, (index + 1) * FR)
            part = lax.dot_general(
                cot,
                pieces[index][FR : 2 * FR, at : at + 256],
                NT,
                preferred_element_type=jnp.float32,
            )
            grads[:, span] = part
            part = probs_ref[pair, :, span] * part
            inner = part if inner is None else inner + part
        inner = jnp.sum(inner, axis=1, keepdims=True)
        inners += [inner[:TB], inner[TB:]]
        acc = None
        for index in range(PIECES):
            span = slice(index * FR, (index + 1) * FR)
            ds = (probs_ref[pair, :, span] * (grads[:, span] - inner)).astype(jnp.bfloat16)
            part = jnp.dot(
                ds, pieces[index][0:FR, at : at + 256], preferred_element_type=jnp.float32
            )
            acc = part if acc is None else acc + part
        grad_q.append(acc)
    gq_ref[...] = (side_by_side(grad_q) * SCALE).astype(jnp.bfloat16)
    band = lax.broadcasted_iota(jnp.int32, (4, TB), 0)
    band = jnp.where(band == 0, start_ref[0, 0], end_ref[0, 0]).astype(jnp.float32)
    sent_ref[2 * TB : 2 * TB + 16] = split(
        jnp.concatenate([norms_ref[...], to_rows(inners)[0:4], band], axis=0)
    )


def spread_kernel(mine_ref, other_ref, out_ref):
    out_ref[...] = jnp.broadcast_to((mine_ref[...] + other_ref[...])[None], (SEQ, 1, W))


def frame_sums(kv_ref, here, tokens):
    totals = []
    extras = [merge(token[2 * TB : 2 * TB + 16]) for token in tokens]
    for pair in range(2):
        at = PAIRS[pair][0]
        keys = kv_ref[0:FR, at : at + 256]
        values = kv_ref[FR : 2 * FR, at : at + 256]
        grad_k = grad_v = None
        for index, extra in enumerate(extras):

            def both(base):
                low = base + 2 * pair
                return jnp.concatenate([extra[low : low + 1], extra[low + 1 : low + 2]], axis=1)

            top, inverse, inner = both(0), both(4), both(8)
            first = jnp.concatenate([extra[12:13]] * 2, axis=1)
            last = jnp.concatenate([extra[13:14]] * 2, axis=1)
            block = blocked(tokens[index][TB : 2 * TB], pair)
            cot = blocked(tokens[index][0:TB], pair)
            scores = (
                lax.dot_general(keys, block, NT, preferred_element_type=jnp.float32) * SCALE
            )
            weights = []
            for half in range(2):
                frame = (2 * here + half).astype(jnp.float32)
                allowed = (frame >= first) & (frame < last)
                weights.append(
                    jnp.exp(scores[half * EB : (half + 1) * EB] - jnp.where(allowed, top, jnp.inf))
                )
            probs = jnp.concatenate(weights, axis=0) * inverse
            grads = lax.dot_general(values, cot, NT, preferred_element_type=jnp.float32)
            ds = (probs * (grads - inner)).astype(jnp.bfloat16)
            part_v = jnp.dot(
                probs.astype(jnp.bfloat16), cot, preferred_element_type=jnp.float32
            )
            part_k = jnp.dot(ds, block, preferred_element_type=jnp.float32)
            if grad_k is None:
                grad_k, grad_v = part_k, part_v
            else:
                grad_k, grad_v = grad_k + part_k, grad_v + part_v
        totals.append((grad_k, grad_v))
    return totals


def columns(totals, which):
    low, high = totals[0][which], totals[1][which]
    return ((0, low[:, :128]), (128, low[:, 128:] + high[:, :128]), (256, high[:, 128:]))


def partner_frame_kernel(kv_ref, sent_ref, below_ref, above_ref, out_ref):
    here = lax.axis_index("seq")
    core = lax.rem(here, 2)
    far = jnp.where(core == 0, above_ref[...], below_ref[...])
    totals = frame_sums(kv_ref, here + 1 - 2 * core, (sent_ref[...], far))
    for which in range(2):
        for at, part in columns(totals, which):
            out_ref[which * FR : (which + 1) * FR, at : at + 128] = part.astype(out_ref.dtype)


def own_frame_kernel(kv_ref, sent_ref, below_ref, above_ref, more_ref, gk_ref, gv_ref):
    tokens = (sent_ref[...], below_ref[...], above_ref[...])
    totals = frame_sums(kv_ref, lax.axis_index("seq"), tokens)
    for which, (out, scale) in enumerate(((gk_ref, SCALE), (gv_ref, 1.0))):
        for at, part in columns(totals, which):
            more = more_ref[which * FR : (which + 1) * FR, at : at + 128].astype(jnp.float32)
            out[:, at : at + 128] = ((part + more) * scale).astype(out.dtype)


VMEM = pl.BlockSpec(memory_space=pltpu.VMEM)
SMEM = pl.BlockSpec(memory_space=pltpu.SMEM)


def call(kernel, outputs, products, scratch=(), scalars=0, vectors=0):
    return pl.pallas_call(
        kernel,
        out_shape=tuple(jax.ShapeDtypeStruct(shape, dtype) for shape, dtype in outputs),
        in_specs=[SMEM] * scalars + [VMEM] * vectors,
        out_specs=(VMEM,) * len(outputs),
        scratch_shapes=[pltpu.VMEM(shape, jnp.float32) for shape in scratch],
        compiler_params=pltpu.CompilerParams(vmem_limit_bytes=24 << 20),
        cost_estimate=pl.CostEstimate(
            flops=products * 2 * 512 * 1280 * 256,
            bytes_accessed=4 << 20,
            transcendentals=512 * 1280,
        ),
    )


def per_device(queries, keys, values, grad_out, gain, band_start, band_end):
    f32, bf16 = jnp.float32, jnp.bfloat16
    here = lax.axis_index("seq")
    core = lax.rem(here, 2)
    own, query, grad, gain_row = pl.pallas_call(
        pack_kernel,
        out_shape=(
            jax.ShapeDtypeStruct((2 * FR, W), bf16),
            jax.ShapeDtypeStruct((TB, W), bf16),
            jax.ShapeDtypeStruct((TB, W), bf16),
            jax.ShapeDtypeStruct((1, W), f32),
        ),
        in_specs=[pl.BlockSpec(memory_space=pltpu.HBM)] * 5,
        out_specs=(VMEM,) * 4,
        scratch_shapes=[pltpu.VMEM((W,), f32), pltpu.SemaphoreType.DMA((5,))],
        compiler_params=pltpu.CompilerParams(vmem_limit_bytes=24 << 20),
        name="pack",
    )(*[
        pltpu.with_memory_space_constraint(array, pltpu.HBM)
        for array in (keys[0], values[0], queries[0], grad_out[0], gain)
    ])
    below = permute(own, "seq", lambda i: i + 2)
    above = permute(own, "seq", lambda i: i - 2)
    partner = permute(own, "seq", lambda i: i ^ 1)
    beyond = permute(jnp.where(core == 0, above, below), "seq", lambda i: i ^ 1)
    pieces = (own, partner, below, above, beyond)
    whole = (2 * TB, PIECES * FR)
    attn, probs, stats, norms = call(
        forward_kernel,
        (((TB, W), f32), ((2, *whole), f32), ((TENSOR, 2, TB), f32), ((8, TB), f32)),
        2,
        scratch=((2, *whole),),
        scalars=2,
        vectors=3 + PIECES,
    )(band_start, band_end, query, grad, gain_row, *pieces)
    stats = lax.all_to_all(stats, "tensor", 0, 0, tiled=False)
    attended, gain_part, grad_queries, sent = call(
        token_kernel,
        (((TB, W), bf16), ((1, W), f32), ((TB, W), bf16), ((2 * TB + 16, W), bf16)),
        2,
        scratch=(whole,),
        scalars=2,
        vectors=7 + PIECES,
    )(band_start, band_end, query, grad, gain_row, attn, probs, norms, stats, *pieces)
    gain_other = lax.ppermute(gain_part, "dp", [(0, 1), (1, 0)])
    tokens = (sent, permute(sent, "seq", lambda i: i + 2), permute(sent, "seq", lambda i: i - 2))
    (gain_both,) = call(spread_kernel, (((SEQ, 1, W), f32),), 0, vectors=2)(gain_part, gain_other)
    spread = lax.all_to_all(gain_both, "seq", 0, 0, tiled=False)
    (to_partner,) = call(
        partner_frame_kernel, (((2 * FR, W), bf16),), 2, vectors=4
    )(partner, *tokens)
    from_partner = permute(to_partner, "seq", lambda i: i ^ 1)
    grad_keys, grad_values = call(
        own_frame_kernel, (((FR, W), bf16), ((FR, W), bf16)), 2, vectors=5
    )(own, *tokens, from_partner)
    grad_gain = jnp.sum(spread, axis=(0, 1))
    return (
        attended[None],
        grad_queries[None],
        grad_keys[None],
        grad_values[None],
        grad_gain,
    )


def solution(mesh):
    return jax.shard_map(
        per_device,
        mesh=mesh,
        in_specs=(
            P("dp", "seq", "tensor"),
            P("dp", "seq", "tensor"),
            P("dp", "seq", "tensor"),
            P("dp", "seq", "tensor"),
            P("tensor"),
            P("dp", "seq"),
            P("dp", "seq"),
        ),
        out_specs=(
            P("dp", "seq", "tensor"),
            P("dp", "seq", "tensor"),
            P("dp", "seq", "tensor"),
            P("dp", "seq", "tensor"),
            P("tensor"),
        ),
        check_vma=False,
    )
```

```python
import jax
import jax.numpy as jnp
from jax import lax
from jax.experimental import pallas as pl
from jax.experimental.pallas import tpu as pltpu
from jax.sharding import PartitionSpec as P


D = 3072
HD = 96
TB = 128
EB = 128
FR = 256
W = 384
TENSOR = 8
SEQ = 32
SCALE = HD ** (-0.5)
epsilon = 1e-06

PIECES = 5
NT = (((1,), (1,)), ((), ()))
PAIRS = ((0, (0, 96)), (128, (64, 160)))


def permute(array, axis, target):
    size = lax.axis_size(axis)
    pairs = [(i, target(i)) for i in range(size) if 0 <= target(i) < size]
    return lax.ppermute(array, axis, pairs)


def offsets(here):
    core = lax.rem(here, 2)
    toward = 1 - 2 * core
    return (0, toward, -2, 2, -toward)


def blocked(rows, pair):
    first, starts = PAIRS[pair]
    part = rows[:, first : first + 256]
    lane = lax.broadcasted_iota(jnp.int32, part.shape, 1)
    zero = jnp.zeros_like(part)
    return jnp.concatenate(
        [jnp.where((lane >= at) & (lane < at + HD), part, zero) for at in starts], axis=0
    )


def side_by_side(pairs):
    lane = lax.broadcasted_iota(jnp.int32, (TB, 256), 1)
    low = jnp.where(lane < HD, pairs[0][:TB], pairs[0][TB:])
    high = jnp.where(lane < 160, pairs[1][:TB], pairs[1][TB:])
    middle = jnp.where(lane[:, :128] < 64, low[:, 128:], high[:, :128])
    return jnp.concatenate([low[:, :128], middle, high[:, 128:]], axis=1)


def to_rows(columns):
    lane = lax.broadcasted_iota(jnp.int32, (TB, TB), 1)
    tile = jnp.zeros((TB, TB), jnp.float32)
    for index, column in enumerate(columns):
        tile = jnp.where(lane == index, column, tile)
    return tile.T


def split(rows):
    terms = []
    for _ in range(3):
        term = rows.astype(jnp.bfloat16)
        rows = rows - term.astype(jnp.float32)
        terms.append(term)
    return jnp.concatenate(terms, axis=1)


def merge(terms):
    terms = terms.astype(jnp.float32)
    return (terms[:, 0:TB] + terms[:, TB : 2 * TB]) + terms[:, 2 * TB : W]


def pack_kernel(
    k_ref, v_ref, q_ref, go_ref, gain_ref, own_ref, query_ref, grad_ref, row_ref, line, sems
):
    moves = (
        (k_ref, own_ref.at[0:FR]),
        (v_ref, own_ref.at[FR : 2 * FR]),
        (q_ref, query_ref),
        (go_ref, grad_ref),
        (gain_ref, line),
    )
    copies = [
        pltpu.make_async_copy(source, target, sems.at[index])
        for index, (source, target) in enumerate(moves)
    ]
    for copy in copies:
        copy.start()
    for copy in copies:
        copy.wait()
    row_ref[...] = line[...].reshape(1, W)


def masked_scores(block, keys, frames, first, last):
    product = lax.dot_general(block, keys, NT, preferred_element_type=jnp.float32) * SCALE
    parts = []
    for half in range(2):
        allowed = (frames + half >= first) & (frames + half < last)
        parts.append(
            product[:, half * EB : (half + 1) * EB] + jnp.where(allowed, 0.0, -jnp.inf)
        )
    return parts


def score_kernel(start_ref, end_ref, q_ref, *rest):
    pieces = rest[: PIECES - 1]
    scores, tops_ref = rest[PIECES - 1 :]
    here = lax.axis_index("seq")
    rows = q_ref[...]
    for pair in range(2):
        at = PAIRS[pair][0]
        block = blocked(rows, pair)
        top = None
        for index, offset in enumerate(offsets(here)[: PIECES - 1]):
            parts = masked_scores(
                block,
                pieces[index][0:FR, at : at + 256],
                2 * (here + offset),
                start_ref[0, 0],
                end_ref[0, 0],
            )
            for half, part in enumerate(parts):
                scores[pair, :, index * FR + half * EB : index * FR + (half + 1) * EB] = part
                top = part if top is None else jnp.maximum(top, part)
        tops_ref[pair] = top


def forward_kernel(
    start_ref, end_ref, q_ref, go_ref, gain_ref, scores_ref, tops_ref, *rest
):
    pieces = rest[:PIECES]
    attn_ref, probs_ref, stats_ref, norms_ref = rest[PIECES:]
    here = lax.axis_index("seq")
    rows = q_ref[...]
    results = []
    tops = []
    scales = []
    for pair in range(2):
        at = PAIRS[pair][0]
        parts = masked_scores(
            blocked(rows, pair),
            pieces[-1][0:FR, at : at + 256],
            2 * (here + offsets(here)[-1]),
            start_ref[0, 0],
            end_ref[0, 0],
        )
        top = jnp.maximum(tops_ref[pair], jnp.maximum(parts[0], parts[1]))
        top = jnp.max(top, axis=1, keepdims=True)
        weights = jnp.concatenate(
            [jnp.exp(scores_ref[pair] - top), *[jnp.exp(part - top) for part in parts]], axis=1
        )
        total = jnp.sum(weights, axis=1, keepdims=True)
        inverse = 1.0 / total
        tops += [top[:TB], top[TB:]]
        scales += [inverse[:TB], inverse[TB:]]
        probs = weights * inverse
        probs_ref[pair] = probs
        probs = probs.astype(jnp.bfloat16)
        acc = None
        for index in range(PIECES):
            part = jnp.dot(
                probs[:, index * FR : (index + 1) * FR],
                pieces[index][FR : 2 * FR, at : at + 256],
                preferred_element_type=jnp.float32,
            )
            acc = part if acc is None else acc + part
        results.append(acc)
    attn = side_by_side(results)
    attn_ref[...] = attn
    scaled = go_ref[...].astype(jnp.float32) * gain_ref[...]
    square = jnp.sum(attn * attn, axis=1, keepdims=True)
    cross = jnp.sum(scaled * attn, axis=1, keepdims=True)
    stats = to_rows([*tops, *scales, square, cross])
    norms_ref[...] = stats[0:8]
    for index in range(TENSOR):
        stats_ref[index] = stats[8:10]


def token_kernel(
    start_ref, end_ref, q_ref, go_ref, gain_ref, attn_ref, probs_ref, norms_ref, stats_ref, *rest
):
    pieces = rest[:PIECES]
    attended_ref, gain_part_ref, gq_ref, sent_ref, grads = rest[PIECES:]
    stats = stats_ref[0]
    for index in range(1, TENSOR):
        stats = stats + stats_ref[index]
    row = lax.broadcasted_iota(jnp.int32, (TB, TB), 0)
    tile = jnp.where(row == 0, stats[0:1], jnp.where(row == 1, stats[1:2], 0.0)).T
    inv = lax.rsqrt(tile[:, 0:1] / D + epsilon)
    mean_cross = inv * tile[:, 1:2] / D
    grad = go_ref[...].astype(jnp.float32)
    gain = gain_ref[...]
    normed = attn_ref[...] * inv
    attended_ref[...] = (normed * gain).astype(jnp.bfloat16)
    gain_part_ref[...] = jnp.broadcast_to(
        jnp.sum(grad * normed, axis=0, keepdims=True)[None], (SEQ, 1, W)
    )
    grad_attn = (inv * (grad * gain - normed * mean_cross)).astype(jnp.bfloat16)
    sent_ref[0:TB] = grad_attn
    grad_q = []
    inners = []
    for pair in range(2):
        at = PAIRS[pair][0]
        cot = blocked(grad_attn, pair)
        inner = None
        for index in range(PIECES):
            span = slice(index * FR, (index + 1) * FR)
            part = lax.dot_general(
                cot,
                pieces[index][FR : 2 * FR, at : at + 256],
                NT,
                preferred_element_type=jnp.float32,
            )
            grads[:, span] = part
            part = probs_ref[pair, :, span] * part
            inner = part if inner is None else inner + part
        inner = jnp.sum(inner, axis=1, keepdims=True)
        inners += [inner[:TB], inner[TB:]]
        acc = None
        for index in range(PIECES):
            span = slice(index * FR, (index + 1) * FR)
            ds = (probs_ref[pair, :, span] * (grads[:, span] - inner)).astype(jnp.bfloat16)
            part = jnp.dot(
                ds, pieces[index][0:FR, at : at + 256], preferred_element_type=jnp.float32
            )
            acc = part if acc is None else acc + part
        grad_q.append(acc)
    gq_ref[...] = (side_by_side(grad_q) * SCALE).astype(jnp.bfloat16)
    band = lax.broadcasted_iota(jnp.int32, (4, TB), 0)
    band = jnp.where(band == 0, start_ref[0, 0], end_ref[0, 0]).astype(jnp.float32)
    sent_ref[TB : TB + 16] = split(
        jnp.concatenate([norms_ref[...], to_rows(inners)[0:4], band], axis=0)
    )


def frame_sums(kv_ref, here, tokens, queries):
    totals = []
    extras = [merge(token[TB : TB + 16]) for token in tokens]
    for pair in range(2):
        at = PAIRS[pair][0]
        keys = kv_ref[0:FR, at : at + 256]
        values = kv_ref[FR : 2 * FR, at : at + 256]
        grad_k = grad_v = None
        for index, extra in enumerate(extras):

            def both(base):
                low = base + 2 * pair
                return jnp.concatenate([extra[low : low + 1], extra[low + 1 : low + 2]], axis=1)

            top, inverse, inner = both(0), both(4), both(8)
            first = jnp.concatenate([extra[12:13]] * 2, axis=1)
            last = jnp.concatenate([extra[13:14]] * 2, axis=1)
            block = blocked(queries[index], pair)
            cot = blocked(tokens[index][0:TB], pair)
            scores = (
                lax.dot_general(keys, block, NT, preferred_element_type=jnp.float32) * SCALE
            )
            weights = []
            for half in range(2):
                frame = (2 * here + half).astype(jnp.float32)
                allowed = (frame >= first) & (frame < last)
                weights.append(
                    jnp.exp(scores[half * EB : (half + 1) * EB] - jnp.where(allowed, top, jnp.inf))
                )
            probs = jnp.concatenate(weights, axis=0) * inverse
            grads = lax.dot_general(values, cot, NT, preferred_element_type=jnp.float32)
            ds = (probs * (grads - inner)).astype(jnp.bfloat16)
            part_v = jnp.dot(
                probs.astype(jnp.bfloat16), cot, preferred_element_type=jnp.float32
            )
            part_k = jnp.dot(ds, block, preferred_element_type=jnp.float32)
            if grad_k is None:
                grad_k, grad_v = part_k, part_v
            else:
                grad_k, grad_v = grad_k + part_k, grad_v + part_v
        totals.append((grad_k, grad_v))
    return totals


def columns(totals, which):
    low, high = totals[0][which], totals[1][which]
    return ((0, low[:, :128]), (128, low[:, 128:] + high[:, :128]), (256, high[:, 128:]))


def partner_frame_kernel(
    kv_ref, sent_ref, below_ref, above_ref, q_ref, q_below_ref, q_above_ref, out_ref
):
    here = lax.axis_index("seq")
    core = lax.rem(here, 2)
    far = jnp.where(core == 0, above_ref[...], below_ref[...])
    q_far = jnp.where(core == 0, q_above_ref[...], q_below_ref[...])
    totals = frame_sums(
        kv_ref, here + 1 - 2 * core, (sent_ref[...], far), (q_ref[...], q_far)
    )
    for which in range(2):
        for at, part in columns(totals, which):
            out_ref[which * FR : (which + 1) * FR, at : at + 128] = part.astype(out_ref.dtype)


def own_frame_kernel(
    kv_ref,
    sent_ref,
    below_ref,
    above_ref,
    q_ref,
    q_below_ref,
    q_above_ref,
    more_ref,
    gk_ref,
    gv_ref,
):
    tokens = (sent_ref[...], below_ref[...], above_ref[...])
    queries = (q_ref[...], q_below_ref[...], q_above_ref[...])
    totals = frame_sums(kv_ref, lax.axis_index("seq"), tokens, queries)
    for which, (out, scale) in enumerate(((gk_ref, SCALE), (gv_ref, 1.0))):
        for at, part in columns(totals, which):
            more = more_ref[which * FR : (which + 1) * FR, at : at + 128].astype(jnp.float32)
            out[:, at : at + 128] = ((part + more) * scale).astype(out.dtype)


VMEM = pl.BlockSpec(memory_space=pltpu.VMEM)
SMEM = pl.BlockSpec(memory_space=pltpu.SMEM)


def call(kernel, outputs, products, scratch=(), scalars=0, vectors=0):
    return pl.pallas_call(
        kernel,
        out_shape=tuple(jax.ShapeDtypeStruct(shape, dtype) for shape, dtype in outputs),
        in_specs=[SMEM] * scalars + [VMEM] * vectors,
        out_specs=(VMEM,) * len(outputs),
        scratch_shapes=[pltpu.VMEM(shape, jnp.float32) for shape in scratch],
        compiler_params=pltpu.CompilerParams(vmem_limit_bytes=24 << 20),
        cost_estimate=pl.CostEstimate(
            flops=products * 2 * 512 * 1280 * 256,
            bytes_accessed=4 << 20,
            transcendentals=512 * 1280,
        ),
    )


def per_device(queries, keys, values, grad_out, gain, band_start, band_end):
    f32, bf16 = jnp.float32, jnp.bfloat16
    here = lax.axis_index("seq")
    core = lax.rem(here, 2)
    own, query, grad, gain_row = pl.pallas_call(
        pack_kernel,
        out_shape=(
            jax.ShapeDtypeStruct((2 * FR, W), bf16),
            jax.ShapeDtypeStruct((TB, W), bf16),
            jax.ShapeDtypeStruct((TB, W), bf16),
            jax.ShapeDtypeStruct((1, W), f32),
        ),
        in_specs=[pl.BlockSpec(memory_space=pltpu.HBM)] * 5,
        out_specs=(VMEM,) * 4,
        scratch_shapes=[pltpu.VMEM((W,), f32), pltpu.SemaphoreType.DMA((5,))],
        compiler_params=pltpu.CompilerParams(vmem_limit_bytes=24 << 20),
        name="pack",
    )(*[
        pltpu.with_memory_space_constraint(array, pltpu.HBM)
        for array in (keys[0], values[0], queries[0], grad_out[0], gain)
    ])
    below = permute(own, "seq", lambda i: i + 2)
    above = permute(own, "seq", lambda i: i - 2)
    partner = permute(own, "seq", lambda i: i ^ 1)
    asked = (query, permute(query, "seq", lambda i: i + 2), permute(query, "seq", lambda i: i - 2))
    whole = (2 * TB, PIECES * FR)
    beyond = permute(jnp.where(core == 0, above, below), "seq", lambda i: i ^ 1)
    pieces = (own, partner, below, above, beyond)
    scores, tops = call(
        score_kernel,
        (((2, 2 * TB, (PIECES - 1) * FR), f32), ((2, 2 * TB, EB), f32)),
        1,
        scalars=2,
        vectors=PIECES,
    )(band_start, band_end, query, *pieces[:-1])
    attn, probs, stats, norms = call(
        forward_kernel,
        (((TB, W), f32), ((2, *whole), f32), ((TENSOR, 2, TB), f32), ((8, TB), f32)),
        1,
        scalars=2,
        vectors=5 + PIECES,
    )(band_start, band_end, query, grad, gain_row, scores, tops, *pieces)
    stats = lax.all_to_all(stats, "tensor", 0, 0, tiled=False)
    attended, gain_part, grad_queries, sent = call(
        token_kernel,
        (((TB, W), bf16), ((SEQ, 1, W), f32), ((TB, W), bf16), ((TB + 16, W), bf16)),
        2,
        scratch=(whole,),
        scalars=2,
        vectors=7 + PIECES,
    )(band_start, band_end, query, grad, gain_row, attn, probs, norms, stats, *pieces)
    spread = lax.all_to_all(gain_part, "seq", 0, 0, tiled=False)
    gain_sum = jnp.sum(spread, axis=(0, 1))
    tokens = (sent, permute(sent, "seq", lambda i: i + 2), permute(sent, "seq", lambda i: i - 2))
    (to_partner,) = call(
        partner_frame_kernel, (((2 * FR, W), bf16),), 2, vectors=7
    )(partner, *tokens, *asked)
    from_partner = permute(to_partner, "seq", lambda i: i ^ 1)
    gain_other = lax.ppermute(gain_sum, "dp", [(0, 1), (1, 0)])
    grad_keys, grad_values = call(
        own_frame_kernel, (((FR, W), bf16), ((FR, W), bf16)), 2, vectors=8
    )(own, *tokens, *asked, from_partner)
    grad_gain = gain_sum + gain_other
    return (
        attended[None],
        grad_queries[None],
        grad_keys[None],
        grad_values[None],
        grad_gain,
    )


def solution(mesh):
    return jax.shard_map(
        per_device,
        mesh=mesh,
        in_specs=(
            P("dp", "seq", "tensor"),
            P("dp", "seq", "tensor"),
            P("dp", "seq", "tensor"),
            P("dp", "seq", "tensor"),
            P("tensor"),
            P("dp", "seq"),
            P("dp", "seq"),
        ),
        out_specs=(
            P("dp", "seq", "tensor"),
            P("dp", "seq", "tensor"),
            P("dp", "seq", "tensor"),
            P("dp", "seq", "tensor"),
            P("tensor"),
        ),
        check_vma=False,
    )
```

```python
import jax
import jax.numpy as jnp
from jax import lax
from jax.experimental import pallas as pl
from jax.experimental.pallas import tpu as pltpu
from jax.sharding import PartitionSpec as P


D = 3072
HD = 96
TB = 128
EB = 128
FR = 256
W = 384
TENSOR = 8
SEQ = 32
SCALE = HD ** (-0.5)
epsilon = 1e-06

PIECES = 5
NT = (((1,), (1,)), ((), ()))
PAIRS = ((0, (0, 96)), (128, (64, 160)))


def permute(array, axis, target):
    size = lax.axis_size(axis)
    pairs = [(i, target(i)) for i in range(size) if 0 <= target(i) < size]
    return lax.ppermute(array, axis, pairs)


def offsets(here):
    core = lax.rem(here, 2)
    toward = 1 - 2 * core
    return (0, toward, -2, 2, -toward)


def blocked(rows, pair):
    first, starts = PAIRS[pair]
    part = rows[:, first : first + 256]
    lane = lax.broadcasted_iota(jnp.int32, part.shape, 1)
    zero = jnp.zeros_like(part)
    return jnp.concatenate(
        [jnp.where((lane >= at) & (lane < at + HD), part, zero) for at in starts], axis=0
    )


def side_by_side(pairs):
    lane = lax.broadcasted_iota(jnp.int32, (TB, 256), 1)
    low = jnp.where(lane < HD, pairs[0][:TB], pairs[0][TB:])
    high = jnp.where(lane < 160, pairs[1][:TB], pairs[1][TB:])
    middle = jnp.where(lane[:, :128] < 64, low[:, 128:], high[:, :128])
    return jnp.concatenate([low[:, :128], middle, high[:, 128:]], axis=1)


def to_rows(columns):
    lane = lax.broadcasted_iota(jnp.int32, (TB, TB), 1)
    tile = jnp.zeros((TB, TB), jnp.float32)
    for index, column in enumerate(columns):
        tile = jnp.where(lane == index, column, tile)
    return tile.T


def split(rows):
    terms = []
    for _ in range(3):
        term = rows.astype(jnp.bfloat16)
        rows = rows - term.astype(jnp.float32)
        terms.append(term)
    return jnp.concatenate(terms, axis=1)


def merge(terms):
    terms = terms.astype(jnp.float32)
    return (terms[:, 0:TB] + terms[:, TB : 2 * TB]) + terms[:, 2 * TB : W]


def pack_kernel(
    k_ref, v_ref, q_ref, go_ref, gain_ref, own_ref, query_ref, grad_ref, row_ref, line, sems
):
    moves = (
        (k_ref, own_ref.at[0:FR]),
        (v_ref, own_ref.at[FR : 2 * FR]),
        (q_ref, query_ref),
        (go_ref, grad_ref),
        (gain_ref, line),
    )
    copies = [
        pltpu.make_async_copy(source, target, sems.at[index])
        for index, (source, target) in enumerate(moves)
    ]
    for copy in copies:
        copy.start()
    for copy in copies:
        copy.wait()
    row_ref[...] = line[...].reshape(1, W)


def masked_scores(block, keys, frames, first, last):
    product = lax.dot_general(block, keys, NT, preferred_element_type=jnp.float32) * SCALE
    parts = []
    for half in range(2):
        allowed = (frames + half >= first) & (frames + half < last)
        parts.append(
            product[:, half * EB : (half + 1) * EB] + jnp.where(allowed, 0.0, -jnp.inf)
        )
    return parts


def score_kernel(start_ref, end_ref, q_ref, *rest):
    pieces = rest[: PIECES - 1]
    scores, tops_ref = rest[PIECES - 1 :]
    here = lax.axis_index("seq")
    rows = q_ref[...]
    for pair in range(2):
        at = PAIRS[pair][0]
        block = blocked(rows, pair)
        top = None
        for index, offset in enumerate(offsets(here)[: PIECES - 1]):
            parts = masked_scores(
                block,
                pieces[index][0:FR, at : at + 256],
                2 * (here + offset),
                start_ref[0, 0],
                end_ref[0, 0],
            )
            for half, part in enumerate(parts):
                scores[pair, :, index * FR + half * EB : index * FR + (half + 1) * EB] = part
                top = part if top is None else jnp.maximum(top, part)
        tops_ref[pair] = top


def forward_kernel(
    start_ref, end_ref, q_ref, go_ref, gain_ref, scores_ref, tops_ref, *rest
):
    pieces = rest[:PIECES]
    attn_ref, probs_ref, stats_ref, norms_ref = rest[PIECES:]
    here = lax.axis_index("seq")
    rows = q_ref[...]
    results = []
    tops = []
    scales = []
    for pair in range(2):
        at = PAIRS[pair][0]
        parts = masked_scores(
            blocked(rows, pair),
            pieces[-1][0:FR, at : at + 256],
            2 * (here + offsets(here)[-1]),
            start_ref[0, 0],
            end_ref[0, 0],
        )
        top = jnp.maximum(tops_ref[pair], jnp.maximum(parts[0], parts[1]))
        top = jnp.max(top, axis=1, keepdims=True)
        weights = jnp.concatenate(
            [jnp.exp(scores_ref[pair] - top), *[jnp.exp(part - top) for part in parts]], axis=1
        )
        total = jnp.sum(weights, axis=1, keepdims=True)
        inverse = 1.0 / total
        tops += [top[:TB], top[TB:]]
        scales += [inverse[:TB], inverse[TB:]]
        probs = weights * inverse
        probs_ref[pair] = probs
        probs = probs.astype(jnp.bfloat16)
        acc = None
        for index in range(PIECES):
            part = jnp.dot(
                probs[:, index * FR : (index + 1) * FR],
                pieces[index][FR : 2 * FR, at : at + 256],
                preferred_element_type=jnp.float32,
            )
            acc = part if acc is None else acc + part
        results.append(acc)
    attn = side_by_side(results)
    attn_ref[...] = attn
    scaled = go_ref[...].astype(jnp.float32) * gain_ref[...]
    square = jnp.sum(attn * attn, axis=1, keepdims=True)
    cross = jnp.sum(scaled * attn, axis=1, keepdims=True)
    stats = to_rows([*tops, *scales, square, cross])
    norms_ref[...] = stats[0:8]
    for index in range(TENSOR):
        stats_ref[index] = stats[8:10]


def token_kernel(
    start_ref, end_ref, q_ref, go_ref, gain_ref, attn_ref, probs_ref, norms_ref, stats_ref, *rest
):
    pieces = rest[:PIECES]
    attended_ref, gain_part_ref, gq_ref, sent_ref, grads = rest[PIECES:]
    stats = stats_ref[0]
    for index in range(1, TENSOR):
        stats = stats + stats_ref[index]
    row = lax.broadcasted_iota(jnp.int32, (TB, TB), 0)
    tile = jnp.where(row == 0, stats[0:1], jnp.where(row == 1, stats[1:2], 0.0)).T
    inv = lax.rsqrt(tile[:, 0:1] / D + epsilon)
    mean_cross = inv * tile[:, 1:2] / D
    grad = go_ref[...].astype(jnp.float32)
    gain = gain_ref[...]
    normed = attn_ref[...] * inv
    attended_ref[...] = (normed * gain).astype(jnp.bfloat16)
    gain_part_ref[...] = jnp.broadcast_to(
        jnp.sum(grad * normed, axis=0, keepdims=True)[None], (SEQ, 1, W)
    )
    grad_attn = (inv * (grad * gain - normed * mean_cross)).astype(jnp.bfloat16)
    rows = q_ref[...]
    sent_ref[0:TB] = grad_attn
    sent_ref[TB : 2 * TB] = rows
    grad_q = []
    inners = []
    for pair in range(2):
        at = PAIRS[pair][0]
        cot = blocked(grad_attn, pair)
        inner = None
        for index in range(PIECES):
            span = slice(index * FR, (index + 1) * FR)
            part = lax.dot_general(
                cot,
                pieces[index][FR : 2 * FR, at : at + 256],
                NT,
                preferred_element_type=jnp.float32,
            )
            grads[:, span] = part
            part = probs_ref[pair, :, span] * part
            inner = part if inner is None else inner + part
        inner = jnp.sum(inner, axis=1, keepdims=True)
        inners += [inner[:TB], inner[TB:]]
        acc = None
        for index in range(PIECES):
            span = slice(index * FR, (index + 1) * FR)
            ds = (probs_ref[pair, :, span] * (grads[:, span] - inner)).astype(jnp.bfloat16)
            part = jnp.dot(
                ds, pieces[index][0:FR, at : at + 256], preferred_element_type=jnp.float32
            )
            acc = part if acc is None else acc + part
        grad_q.append(acc)
    gq_ref[...] = (side_by_side(grad_q) * SCALE).astype(jnp.bfloat16)
    band = lax.broadcasted_iota(jnp.int32, (4, TB), 0)
    band = jnp.where(band == 0, start_ref[0, 0], end_ref[0, 0]).astype(jnp.float32)
    sent_ref[2 * TB : 2 * TB + 16] = split(
        jnp.concatenate([norms_ref[...], to_rows(inners)[0:4], band], axis=0)
    )


def frame_sums(kv_ref, here, tokens):
    totals = []
    extras = [merge(token[2 * TB : 2 * TB + 16]) for token in tokens]
    for pair in range(2):
        at = PAIRS[pair][0]
        keys = kv_ref[0:FR, at : at + 256]
        values = kv_ref[FR : 2 * FR, at : at + 256]
        grad_k = grad_v = None
        for index, extra in enumerate(extras):

            def both(base):
                low = base + 2 * pair
                return jnp.concatenate([extra[low : low + 1], extra[low + 1 : low + 2]], axis=1)

            top, inverse, inner = both(0), both(4), both(8)
            first = jnp.concatenate([extra[12:13]] * 2, axis=1)
            last = jnp.concatenate([extra[13:14]] * 2, axis=1)
            block = blocked(tokens[index][TB : 2 * TB], pair)
            cot = blocked(tokens[index][0:TB], pair)
            scores = (
                lax.dot_general(keys, block, NT, preferred_element_type=jnp.float32) * SCALE
            )
            weights = []
            for half in range(2):
                frame = (2 * here + half).astype(jnp.float32)
                allowed = (frame >= first) & (frame < last)
                weights.append(
                    jnp.exp(scores[half * EB : (half + 1) * EB] - jnp.where(allowed, top, jnp.inf))
                )
            probs = jnp.concatenate(weights, axis=0) * inverse
            grads = lax.dot_general(values, cot, NT, preferred_element_type=jnp.float32)
            ds = (probs * (grads - inner)).astype(jnp.bfloat16)
            part_v = jnp.dot(
                probs.astype(jnp.bfloat16), cot, preferred_element_type=jnp.float32
            )
            part_k = jnp.dot(ds, block, preferred_element_type=jnp.float32)
            if grad_k is None:
                grad_k, grad_v = part_k, part_v
            else:
                grad_k, grad_v = grad_k + part_k, grad_v + part_v
        totals.append((grad_k, grad_v))
    return totals


def columns(totals, which):
    low, high = totals[0][which], totals[1][which]
    return ((0, low[:, :128]), (128, low[:, 128:] + high[:, :128]), (256, high[:, 128:]))


def partner_frame_kernel(kv_ref, sent_ref, below_ref, above_ref, out_ref):
    here = lax.axis_index("seq")
    core = lax.rem(here, 2)
    far = jnp.where(core == 0, above_ref[...], below_ref[...])
    totals = frame_sums(kv_ref, here + 1 - 2 * core, (sent_ref[...], far))
    for which in range(2):
        for at, part in columns(totals, which):
            out_ref[which * FR : (which + 1) * FR, at : at + 128] = part.astype(out_ref.dtype)


def own_frame_kernel(kv_ref, sent_ref, below_ref, above_ref, more_ref, gk_ref, gv_ref):
    tokens = (sent_ref[...], below_ref[...], above_ref[...])
    totals = frame_sums(kv_ref, lax.axis_index("seq"), tokens)
    for which, (out, scale) in enumerate(((gk_ref, SCALE), (gv_ref, 1.0))):
        for at, part in columns(totals, which):
            more = more_ref[which * FR : (which + 1) * FR, at : at + 128].astype(jnp.float32)
            out[:, at : at + 128] = ((part + more) * scale).astype(out.dtype)


VMEM = pl.BlockSpec(memory_space=pltpu.VMEM)
SMEM = pl.BlockSpec(memory_space=pltpu.SMEM)


def call(kernel, outputs, products, scratch=(), scalars=0, vectors=0):
    return pl.pallas_call(
        kernel,
        out_shape=tuple(jax.ShapeDtypeStruct(shape, dtype) for shape, dtype in outputs),
        in_specs=[SMEM] * scalars + [VMEM] * vectors,
        out_specs=(VMEM,) * len(outputs),
        scratch_shapes=[pltpu.VMEM(shape, jnp.float32) for shape in scratch],
        compiler_params=pltpu.CompilerParams(vmem_limit_bytes=24 << 20),
        cost_estimate=pl.CostEstimate(
            flops=products * 2 * 512 * 1280 * 256,
            bytes_accessed=4 << 20,
            transcendentals=512 * 1280,
        ),
    )


def per_device(queries, keys, values, grad_out, gain, band_start, band_end):
    f32, bf16 = jnp.float32, jnp.bfloat16
    here = lax.axis_index("seq")
    core = lax.rem(here, 2)
    own, query, grad, gain_row = pl.pallas_call(
        pack_kernel,
        out_shape=(
            jax.ShapeDtypeStruct((2 * FR, W), bf16),
            jax.ShapeDtypeStruct((TB, W), bf16),
            jax.ShapeDtypeStruct((TB, W), bf16),
            jax.ShapeDtypeStruct((1, W), f32),
        ),
        in_specs=[pl.BlockSpec(memory_space=pltpu.HBM)] * 5,
        out_specs=(VMEM,) * 4,
        scratch_shapes=[pltpu.VMEM((W,), f32), pltpu.SemaphoreType.DMA((5,))],
        compiler_params=pltpu.CompilerParams(vmem_limit_bytes=24 << 20),
        name="pack",
    )(*[
        pltpu.with_memory_space_constraint(array, pltpu.HBM)
        for array in (keys[0], values[0], queries[0], grad_out[0], gain)
    ])
    below = permute(own, "seq", lambda i: i + 2)
    above = permute(own, "seq", lambda i: i - 2)
    partner = permute(own, "seq", lambda i: i ^ 1)
    whole = (2 * TB, PIECES * FR)
    beyond = permute(jnp.where(core == 0, above, below), "seq", lambda i: i ^ 1)
    pieces = (own, partner, below, above, beyond)
    scores, tops = call(
        score_kernel,
        (((2, 2 * TB, (PIECES - 1) * FR), f32), ((2, 2 * TB, EB), f32)),
        1,
        scalars=2,
        vectors=PIECES,
    )(band_start, band_end, query, *pieces[:-1])
    attn, probs, stats, norms = call(
        forward_kernel,
        (((TB, W), f32), ((2, *whole), f32), ((TENSOR, 2, TB), f32), ((8, TB), f32)),
        1,
        scalars=2,
        vectors=5 + PIECES,
    )(band_start, band_end, query, grad, gain_row, scores, tops, *pieces)
    stats = lax.all_to_all(stats, "tensor", 0, 0, tiled=False)
    attended, gain_part, grad_queries, sent = call(
        token_kernel,
        (((TB, W), bf16), ((SEQ, 1, W), f32), ((TB, W), bf16), ((2 * TB + 16, W), bf16)),
        2,
        scratch=(whole,),
        scalars=2,
        vectors=7 + PIECES,
    )(band_start, band_end, query, grad, gain_row, attn, probs, norms, stats, *pieces)
    spread = lax.all_to_all(gain_part, "seq", 0, 0, tiled=False)
    gain_sum = jnp.sum(spread, axis=(0, 1))
    tokens_below = permute(sent, "seq", lambda i: i + 2)
    tokens_above = permute(sent, "seq", lambda i: i - 2)
    tokens = (sent, tokens_below, tokens_above)
    (to_partner,) = call(
        partner_frame_kernel, (((2 * FR, W), bf16),), 2, vectors=4
    )(partner, *tokens)
    from_partner = permute(to_partner, "seq", lambda i: i ^ 1)
    gain_other = lax.ppermute(gain_sum, "dp", [(0, 1), (1, 0)])
    grad_keys, grad_values = call(
        own_frame_kernel, (((FR, W), bf16), ((FR, W), bf16)), 2, vectors=5
    )(own, *tokens, from_partner)
    grad_gain = gain_sum + gain_other
    return (
        attended[None],
        grad_queries[None],
        grad_keys[None],
        grad_values[None],
        grad_gain,
    )


def solution(mesh):
    return jax.shard_map(
        per_device,
        mesh=mesh,
        in_specs=(
            P("dp", "seq", "tensor"),
            P("dp", "seq", "tensor"),
            P("dp", "seq", "tensor"),
            P("dp", "seq", "tensor"),
            P("tensor"),
            P("dp", "seq"),
            P("dp", "seq"),
        ),
        out_specs=(
            P("dp", "seq", "tensor"),
            P("dp", "seq", "tensor"),
            P("dp", "seq", "tensor"),
            P("dp", "seq", "tensor"),
            P("tensor"),
        ),
        check_vma=False,
    )
```

```python
import jax
import jax.numpy as jnp
from jax import lax
from jax.experimental import pallas as pl
from jax.experimental.pallas import tpu as pltpu
from jax.sharding import PartitionSpec as P


D = 3072
HD = 96
TB = 128
EB = 128
FR = 256
W = 384
TENSOR = 8
SEQ = 32
SCALE = HD ** (-0.5)
epsilon = 1e-06

PIECES = 5
NT = (((1,), (1,)), ((), ()))
PAIRS = ((0, (0, 96)), (128, (64, 160)))


def permute(array, axis, target):
    size = lax.axis_size(axis)
    pairs = [(i, target(i)) for i in range(size) if 0 <= target(i) < size]
    return lax.ppermute(array, axis, pairs)


def offsets(here):
    core = lax.rem(here, 2)
    toward = 1 - 2 * core
    return (0, toward, -2, 2, -toward)


def blocked(rows, pair):
    first, starts = PAIRS[pair]
    part = rows[:, first : first + 256]
    lane = lax.broadcasted_iota(jnp.int32, part.shape, 1)
    zero = jnp.zeros_like(part)
    return jnp.concatenate(
        [jnp.where((lane >= at) & (lane < at + HD), part, zero) for at in starts], axis=0
    )


def side_by_side(pairs):
    lane = lax.broadcasted_iota(jnp.int32, (TB, 256), 1)
    low = jnp.where(lane < HD, pairs[0][:TB], pairs[0][TB:])
    high = jnp.where(lane < 160, pairs[1][:TB], pairs[1][TB:])
    middle = jnp.where(lane[:, :128] < 64, low[:, 128:], high[:, :128])
    return jnp.concatenate([low[:, :128], middle, high[:, 128:]], axis=1)


def to_rows(columns):
    lane = lax.broadcasted_iota(jnp.int32, (TB, TB), 1)
    tile = jnp.zeros((TB, TB), jnp.float32)
    for index, column in enumerate(columns):
        tile = jnp.where(lane == index, column, tile)
    return tile.T


def split(rows):
    terms = []
    for _ in range(3):
        term = rows.astype(jnp.bfloat16)
        rows = rows - term.astype(jnp.float32)
        terms.append(term)
    return jnp.concatenate(terms, axis=1)


def merge(terms):
    terms = terms.astype(jnp.float32)
    return (terms[:, 0:TB] + terms[:, TB : 2 * TB]) + terms[:, 2 * TB : W]


def pack_kernel(
    k_ref, v_ref, q_ref, go_ref, gain_ref, own_ref, query_ref, grad_ref, row_ref, line, sems
):
    moves = (
        (k_ref, own_ref.at[0:FR]),
        (v_ref, own_ref.at[FR : 2 * FR]),
        (q_ref, query_ref),
        (go_ref, grad_ref),
        (gain_ref, line),
    )
    copies = [
        pltpu.make_async_copy(source, target, sems.at[index])
        for index, (source, target) in enumerate(moves)
    ]
    for copy in copies:
        copy.start()
    for copy in copies:
        copy.wait()
    row_ref[...] = line[...].reshape(1, W)


def masked_scores(block, keys, frames, first, last):
    product = lax.dot_general(block, keys, NT, preferred_element_type=jnp.float32) * SCALE
    parts = []
    for half in range(2):
        allowed = (frames + half >= first) & (frames + half < last)
        parts.append(
            product[:, half * EB : (half + 1) * EB] + jnp.where(allowed, 0.0, -jnp.inf)
        )
    return parts


def score_kernel(start_ref, end_ref, q_ref, *rest):
    pieces = rest[: PIECES - 1]
    scores, tops_ref = rest[PIECES - 1 :]
    here = lax.axis_index("seq")
    rows = q_ref[...]
    for pair in range(2):
        at = PAIRS[pair][0]
        block = blocked(rows, pair)
        top = None
        for index, offset in enumerate(offsets(here)[: PIECES - 1]):
            parts = masked_scores(
                block,
                pieces[index][0:FR, at : at + 256],
                2 * (here + offset),
                start_ref[0, 0],
                end_ref[0, 0],
            )
            for half, part in enumerate(parts):
                scores[pair, :, index * FR + half * EB : index * FR + (half + 1) * EB] = part
                top = part if top is None else jnp.maximum(top, part)
        tops_ref[pair] = top


def forward_kernel(
    start_ref, end_ref, q_ref, go_ref, gain_ref, scores_ref, tops_ref, *rest
):
    pieces = rest[:PIECES]
    attn_ref, probs_ref, stats_ref, norms_ref = rest[PIECES:]
    here = lax.axis_index("seq")
    rows = q_ref[...]
    results = []
    tops = []
    scales = []
    for pair in range(2):
        at = PAIRS[pair][0]
        parts = masked_scores(
            blocked(rows, pair),
            pieces[-1][0:FR, at : at + 256],
            2 * (here + offsets(here)[-1]),
            start_ref[0, 0],
            end_ref[0, 0],
        )
        top = jnp.maximum(tops_ref[pair], jnp.maximum(parts[0], parts[1]))
        top = jnp.max(top, axis=1, keepdims=True)
        weights = jnp.concatenate(
            [jnp.exp(scores_ref[pair] - top), *[jnp.exp(part - top) for part in parts]], axis=1
        )
        total = jnp.sum(weights, axis=1, keepdims=True)
        inverse = 1.0 / total
        tops += [top[:TB], top[TB:]]
        scales += [inverse[:TB], inverse[TB:]]
        probs = weights * inverse
        probs_ref[pair] = probs
        probs = probs.astype(jnp.bfloat16)
        acc = None
        for index in range(PIECES):
            part = jnp.dot(
                probs[:, index * FR : (index + 1) * FR],
                pieces[index][FR : 2 * FR, at : at + 256],
                preferred_element_type=jnp.float32,
            )
            acc = part if acc is None else acc + part
        results.append(acc)
    attn = side_by_side(results)
    attn_ref[...] = attn
    scaled = go_ref[...].astype(jnp.float32) * gain_ref[...]
    square = jnp.sum(attn * attn, axis=1, keepdims=True)
    cross = jnp.sum(scaled * attn, axis=1, keepdims=True)
    stats = to_rows([*tops, *scales, square, cross])
    norms_ref[...] = stats[0:8]
    for index in range(TENSOR):
        stats_ref[index] = stats[8:10]


def token_kernel(
    start_ref, end_ref, q_ref, go_ref, gain_ref, attn_ref, probs_ref, norms_ref, stats_ref, *rest
):
    pieces = rest[:PIECES]
    attended_ref, gain_part_ref, gq_ref, sent_ref, grads = rest[PIECES:]
    stats = stats_ref[0]
    for index in range(1, TENSOR):
        stats = stats + stats_ref[index]
    row = lax.broadcasted_iota(jnp.int32, (TB, TB), 0)
    tile = jnp.where(row == 0, stats[0:1], jnp.where(row == 1, stats[1:2], 0.0)).T
    inv = lax.rsqrt(tile[:, 0:1] / D + epsilon)
    mean_cross = inv * tile[:, 1:2] / D
    grad = go_ref[...].astype(jnp.float32)
    gain = gain_ref[...]
    normed = attn_ref[...] * inv
    attended_ref[...] = (normed * gain).astype(jnp.bfloat16)
    gain_part_ref[...] = jnp.broadcast_to(
        jnp.sum(grad * normed, axis=0, keepdims=True)[None], (SEQ, 1, W)
    )
    grad_attn = (inv * (grad * gain - normed * mean_cross)).astype(jnp.bfloat16)
    sent_ref[0:TB] = grad_attn
    grad_q = []
    inners = []
    for pair in range(2):
        at = PAIRS[pair][0]
        cot = blocked(grad_attn, pair)
        inner = None
        for index in range(PIECES):
            span = slice(index * FR, (index + 1) * FR)
            part = lax.dot_general(
                cot,
                pieces[index][FR : 2 * FR, at : at + 256],
                NT,
                preferred_element_type=jnp.float32,
            )
            grads[:, span] = part
            part = probs_ref[pair, :, span] * part
            inner = part if inner is None else inner + part
        inner = jnp.sum(inner, axis=1, keepdims=True)
        inners += [inner[:TB], inner[TB:]]
        acc = None
        for index in range(PIECES):
            span = slice(index * FR, (index + 1) * FR)
            ds = (probs_ref[pair, :, span] * (grads[:, span] - inner)).astype(jnp.bfloat16)
            part = jnp.dot(
                ds, pieces[index][0:FR, at : at + 256], preferred_element_type=jnp.float32
            )
            acc = part if acc is None else acc + part
        grad_q.append(acc)
    gq_ref[...] = (side_by_side(grad_q) * SCALE).astype(jnp.bfloat16)
    band = lax.broadcasted_iota(jnp.int32, (4, TB), 0)
    band = jnp.where(band == 0, start_ref[0, 0], end_ref[0, 0]).astype(jnp.float32)
    sent_ref[TB : TB + 16] = split(
        jnp.concatenate([norms_ref[...], to_rows(inners)[0:4], band], axis=0)
    )


def frame_sums(kv_ref, here, tokens, queries):
    totals = []
    extras = [merge(token[TB : TB + 16]) for token in tokens]
    for pair in range(2):
        at = PAIRS[pair][0]
        keys = kv_ref[0:FR, at : at + 256]
        values = kv_ref[FR : 2 * FR, at : at + 256]
        grad_k = grad_v = None
        for index, extra in enumerate(extras):

            def both(base):
                low = base + 2 * pair
                return jnp.concatenate([extra[low : low + 1], extra[low + 1 : low + 2]], axis=1)

            top, inverse, inner = both(0), both(4), both(8)
            first = jnp.concatenate([extra[12:13]] * 2, axis=1)
            last = jnp.concatenate([extra[13:14]] * 2, axis=1)
            block = blocked(queries[index], pair)
            cot = blocked(tokens[index][0:TB], pair)
            scores = (
                lax.dot_general(keys, block, NT, preferred_element_type=jnp.float32) * SCALE
            )
            weights = []
            for half in range(2):
                frame = (2 * here + half).astype(jnp.float32)
                allowed = (frame >= first) & (frame < last)
                weights.append(
                    jnp.exp(scores[half * EB : (half + 1) * EB] - jnp.where(allowed, top, jnp.inf))
                )
            probs = jnp.concatenate(weights, axis=0) * inverse
            grads = lax.dot_general(values, cot, NT, preferred_element_type=jnp.float32)
            ds = (probs * (grads - inner)).astype(jnp.bfloat16)
            part_v = jnp.dot(
                probs.astype(jnp.bfloat16), cot, preferred_element_type=jnp.float32
            )
            part_k = jnp.dot(ds, block, preferred_element_type=jnp.float32)
            if grad_k is None:
                grad_k, grad_v = part_k, part_v
            else:
                grad_k, grad_v = grad_k + part_k, grad_v + part_v
        totals.append((grad_k, grad_v))
    return totals


def columns(totals, which):
    low, high = totals[0][which], totals[1][which]
    return ((0, low[:, :128]), (128, low[:, 128:] + high[:, :128]), (256, high[:, 128:]))


def partner_frame_kernel(
    kv_ref, sent_ref, below_ref, above_ref, q_ref, q_below_ref, q_above_ref, out_ref
):
    here = lax.axis_index("seq")
    core = lax.rem(here, 2)
    far = jnp.where(core == 0, above_ref[...], below_ref[...])
    q_far = jnp.where(core == 0, q_above_ref[...], q_below_ref[...])
    totals = frame_sums(
        kv_ref, here + 1 - 2 * core, (sent_ref[...], far), (q_ref[...], q_far)
    )
    for which in range(2):
        for at, part in columns(totals, which):
            out_ref[which * FR : (which + 1) * FR, at : at + 128] = part.astype(out_ref.dtype)


def own_frame_kernel(
    kv_ref,
    sent_ref,
    below_ref,
    above_ref,
    q_ref,
    q_below_ref,
    q_above_ref,
    more_ref,
    gk_ref,
    gv_ref,
):
    tokens = (sent_ref[...], below_ref[...], above_ref[...])
    queries = (q_ref[...], q_below_ref[...], q_above_ref[...])
    totals = frame_sums(kv_ref, lax.axis_index("seq"), tokens, queries)
    for which, (out, scale) in enumerate(((gk_ref, SCALE), (gv_ref, 1.0))):
        for at, part in columns(totals, which):
            more = more_ref[which * FR : (which + 1) * FR, at : at + 128].astype(jnp.float32)
            out[:, at : at + 128] = ((part + more) * scale).astype(out.dtype)


VMEM = pl.BlockSpec(memory_space=pltpu.VMEM)
SMEM = pl.BlockSpec(memory_space=pltpu.SMEM)


def call(kernel, outputs, products, scratch=(), scalars=0, vectors=0):
    return pl.pallas_call(
        kernel,
        out_shape=tuple(jax.ShapeDtypeStruct(shape, dtype) for shape, dtype in outputs),
        in_specs=[SMEM] * scalars + [VMEM] * vectors,
        out_specs=(VMEM,) * len(outputs),
        scratch_shapes=[pltpu.VMEM(shape, jnp.float32) for shape in scratch],
        compiler_params=pltpu.CompilerParams(vmem_limit_bytes=24 << 20),
        cost_estimate=pl.CostEstimate(
            flops=products * 2 * 512 * 1280 * 256,
            bytes_accessed=4 << 20,
            transcendentals=512 * 1280,
        ),
    )


def per_device(queries, keys, values, grad_out, gain, band_start, band_end):
    f32, bf16 = jnp.float32, jnp.bfloat16
    here = lax.axis_index("seq")
    core = lax.rem(here, 2)
    own, query, grad, gain_row = pl.pallas_call(
        pack_kernel,
        out_shape=(
            jax.ShapeDtypeStruct((2 * FR, W), bf16),
            jax.ShapeDtypeStruct((TB, W), bf16),
            jax.ShapeDtypeStruct((TB, W), bf16),
            jax.ShapeDtypeStruct((1, W), f32),
        ),
        in_specs=[pl.BlockSpec(memory_space=pltpu.HBM)] * 5,
        out_specs=(VMEM,) * 4,
        scratch_shapes=[pltpu.VMEM((W,), f32), pltpu.SemaphoreType.DMA((5,))],
        compiler_params=pltpu.CompilerParams(vmem_limit_bytes=24 << 20),
        name="pack",
    )(*[
        pltpu.with_memory_space_constraint(array, pltpu.HBM)
        for array in (keys[0], values[0], queries[0], grad_out[0], gain)
    ])
    above = permute(own, "seq", lambda i: i - 2)
    below = permute(own, "seq", lambda i: i + 2)
    partner = permute(own, "seq", lambda i: i ^ 1)
    asked_above = permute(query, "seq", lambda i: i - 2)
    asked_below = permute(query, "seq", lambda i: i + 2)
    asked = (query, asked_below, asked_above)
    whole = (2 * TB, PIECES * FR)
    beyond = permute(jnp.where(core == 0, above, below), "seq", lambda i: i ^ 1)
    pieces = (own, partner, below, above, beyond)
    scores, tops = call(
        score_kernel,
        (((2, 2 * TB, (PIECES - 1) * FR), f32), ((2, 2 * TB, EB), f32)),
        1,
        scalars=2,
        vectors=PIECES,
    )(band_start, band_end, query, *pieces[:-1])
    attn, probs, stats, norms = call(
        forward_kernel,
        (((TB, W), f32), ((2, *whole), f32), ((TENSOR, 2, TB), f32), ((8, TB), f32)),
        1,
        scalars=2,
        vectors=5 + PIECES,
    )(band_start, band_end, query, grad, gain_row, scores, tops, *pieces)
    stats = lax.all_to_all(stats, "tensor", 0, 0, tiled=False)
    attended, gain_part, grad_queries, sent = call(
        token_kernel,
        (((TB, W), bf16), ((SEQ, 1, W), f32), ((TB, W), bf16), ((TB + 16, W), bf16)),
        2,
        scratch=(whole,),
        scalars=2,
        vectors=7 + PIECES,
    )(band_start, band_end, query, grad, gain_row, attn, probs, norms, stats, *pieces)
    spread = lax.all_to_all(gain_part, "seq", 0, 0, tiled=False)
    gain_sum = jnp.sum(spread, axis=(0, 1))
    tokens_above = permute(sent, "seq", lambda i: i - 2)
    tokens_below = permute(sent, "seq", lambda i: i + 2)
    tokens = (sent, tokens_below, tokens_above)
    (to_partner,) = call(
        partner_frame_kernel, (((2 * FR, W), bf16),), 2, vectors=7
    )(partner, *tokens, *asked)
    from_partner = permute(to_partner, "seq", lambda i: i ^ 1)
    gain_other = lax.ppermute(gain_sum, "dp", [(0, 1), (1, 0)])
    grad_keys, grad_values = call(
        own_frame_kernel, (((FR, W), bf16), ((FR, W), bf16)), 2, vectors=8
    )(own, *tokens, *asked, from_partner)
    grad_gain = gain_sum + gain_other
    return (
        attended[None],
        grad_queries[None],
        grad_keys[None],
        grad_values[None],
        grad_gain,
    )


def solution(mesh):
    return jax.shard_map(
        per_device,
        mesh=mesh,
        in_specs=(
            P("dp", "seq", "tensor"),
            P("dp", "seq", "tensor"),
            P("dp", "seq", "tensor"),
            P("dp", "seq", "tensor"),
            P("tensor"),
            P("dp", "seq"),
            P("dp", "seq"),
        ),
        out_specs=(
            P("dp", "seq", "tensor"),
            P("dp", "seq", "tensor"),
            P("dp", "seq", "tensor"),
            P("dp", "seq", "tensor"),
            P("tensor"),
        ),
        check_vma=False,
    )
```
